32 devices in a mesh: stream: 4 (over z), trans: 8 (over y, x, core).
Axes of the slice: x: 2, y: 2, z: 4, core: 2. Of those that a mesh axis runs over, the one named last changes fastest.
Arguments:
- rhs: float32 [64, 128, 128], P('stream', 'trans'), may hold values from -60 to 60
- vof: int32 [64, 128, 128], P('stream', 'trans'), may hold values from 0 to 1000
- disc_owner: int32 [4, 2048, 1], P('stream', 'trans'), may hold values from 0 to 7; in each aligned block of 256 rows (0 to 255, 256 to 511, ..., all dimensions but the last counted through in order) at most 32 rows name the same one
- disc_cell: int32 [4, 2048], P('stream', 'trans'), may hold values from 0 to 32767
- disc_force: float32 [4, 2048], P('stream', 'trans'), may hold values from -240 to 240
Outputs:
- pressure: float32 [64, 128, 128], P('stream', 'trans')
The draws below stay inside these ranges and needn't reach their ends.
Inputs may be any that keep to these rules, and one draw needn't show every extreme that they name: `disc_owner`: among the 256 rows of one device at most 32 name the same owner, and on some device exactly 32 rows name one owner.
All inputs are finite; a program needn't handle non-finite values.
Results may differ from the reference program's by a relative error of at most 0.0001.
Values sent between devices are 32-bit elements; how exact they have to be, the bound alone decides.
No kernel may reach another device: no remote copies, remote signals or barrier semaphores. Data moves between devices by JAX's collectives and lax.ppermute only.
A program may use at most 192 MiB of HBM per device.

```python
import math
import jax
import jax.numpy as jnp
import numpy as np

CX = 16
CY = 16
CZ = 128
LEVELS = 4
PRE = 2
POST = 2
CSWEEPS = 8
DISC_DEV = 256
CAP = 32
SLABS = 4
DISC_ROWS = 2048
NX = 64
NY = 128
N_TRANS = 8


def plant(values, key, least, high):
    extent = values.shape
    place = [jax.random.randint(jax.random.fold_in(key, axis), (), 0, extent[axis]) for axis in range(len(extent))]
    values = values.at[tuple(place)].set(least)
    longest = extent.index(max(extent))
    place[longest] = (place[longest] + 1) % extent[longest]
    return values.at[tuple(place)].set(high)


def level_of(own_key, shape, cuts, smallest, high):
    gain = 1.0
    for dim, shards_of in cuts:
        draws = jax.random.uniform(jax.random.fold_in(jax.random.fold_in(own_key, 6), dim), (shards_of,), jnp.float32, smallest / len(cuts), high / len(cuts))
        gain = gain * jnp.repeat(jnp.exp(draws), shape[dim] // shards_of).reshape((-1,) + (1,) * (len(shape) - 1 - dim))
    return gain


def shared_out(rng, own, number, rows, number_of, top, reach, slope):
    sequence = jax.random.permutation(rng, number_of)
    packed, usual = portions_of(number_of, rows * top, reach, slope, True), portions_of(number_of, rows * top, reach, slope, False)
    places = jnp.arange(number_of)

    def named(lengths, rotation):
        used = int((lengths > 0).sum())
        fixed = max(1, used // 4)
        shifted = fixed + (places - fixed + rotation * (used - fixed)) % max(1, number_of - fixed)
        return jnp.zeros((number_of,), jnp.int32).at[sequence[jnp.where(places < fixed, places, shifted)]].set(jnp.asarray(lengths, jnp.int32))

    lengths = jnp.where(number % 4 == 0, named(packed, number // 4), named(usual, number - number // 4 - 1))
    mixed = jax.random.permutation(jax.random.fold_in(own, 3), number_of)
    giver, taker = mixed[0:number_of // 2 * 2:2], mixed[1:number_of // 2 * 2:2]
    margin = jnp.minimum(lengths[giver] - 1, reach - lengths[taker]) // 2
    margin = jnp.where((giver == sequence[0]) | (taker == sequence[0]) | (lengths[taker] == 0), 0, jnp.maximum(margin, 0))
    shifted = jax.random.randint(jax.random.fold_in(own, 4), (number_of // 2,), 0, 1 << 20) % (margin + 1)
    lengths = lengths.at[giver].add(-shifted).at[taker].add(shifted)
    items = jnp.searchsorted(jnp.cumsum(lengths), jnp.arange(rows * top), side="right").astype(jnp.int32)
    listing = items.reshape(top, rows).T
    listing = listing[jax.random.permutation(jax.random.fold_in(own, 1), rows)]
    rotation = jax.random.randint(jax.random.fold_in(own, 2), (rows, 1), 0, top)
    return jnp.take_along_axis(listing, (jnp.arange(top)[None, :] + rotation) % top, axis=1)


def portions_of(amount, total, most, lean, full):
    loads = [(1 << 20) // math.isqrt(standing ** lean) + 1 for standing in range(1, amount + 1)]
    largest = most if full else min(most, max(-(-total // amount), total * loads[0] // sum(loads)))
    least = 1 if total - largest >= amount - 1 else 0
    given, rest = [largest] + [least] * (amount - 1), total - largest - least * (amount - 1)
    while rest > 0:
        free = [i for i in range(1, amount) if given[i] < largest] or [i for i in range(1, amount) if given[i] < most]
        pool, budget = sum([loads[i] for i in free]), rest
        for i in free:
            extra = min(most - given[i], max(1, budget * loads[i] // pool), rest)
            given[i] = given[i] + extra
            rest = rest - extra
    return np.array(given)


def gaussian(rng, shape, deviation, reach, pieces=(), held_as=jnp.bfloat16):
    gain = level_of(rng, shape, pieces, -0.22, 0.18) if pieces else 1.0
    drawn = jax.random.normal(rng, shape, jnp.float32) * deviation * gain
    return jnp.minimum(jnp.maximum(drawn, -reach), reach).astype(held_as)


def setup_inputs(seed: int = 0) -> dict:
    splits = jax.random.split(jax.random.key(seed), 6)
    rhs = gaussian(splits[0], (NX, NY, CZ), 10.0, 60.0, ((0, 4), (1, 8)), jnp.float32)
    vof = plant(jax.random.randint(splits[1], (NX, NY, CZ), 0, 1001), jax.random.fold_in(splits[1], 1), 0, 1000).astype(jnp.int32)
    disc_owner_keys = jax.random.split(jax.random.fold_in(splits[2], 1), SLABS * DISC_ROWS // DISC_DEV)
    disc_owner_turns = jax.random.permutation(jax.random.fold_in(splits[2], 3), SLABS * DISC_ROWS // DISC_DEV)
    disc_owner = jax.vmap(lambda own, number: shared_out(jax.random.fold_in(splits[2], 2), own, number, DISC_DEV, N_TRANS, 1, CAP, 2))(disc_owner_keys, disc_owner_turns).reshape((SLABS, DISC_ROWS, 1))
    disc_cell = plant(jax.random.randint(splits[3], (SLABS, DISC_ROWS), 0, CX * CY * CZ), jax.random.fold_in(splits[3], 1), 0, (CX * CY * CZ) - 1).astype(jnp.int32)
    disc_force = gaussian(splits[4], (SLABS, DISC_ROWS), 40.0, 240.0, ((0, 4), (1, 8)), jnp.float32)
    return {"rhs": rhs, "vof": vof, "disc_owner": disc_owner, "disc_cell": disc_cell, "disc_force": disc_force}


air_density = 0.0012
omega_factor = 0.8


def neighbour_slices(padded):
    return (padded[2:, 1:-1, 1:-1], padded[:-2, 1:-1, 1:-1], padded[1:-1, 2:, 1:-1],
            padded[1:-1, :-2, 1:-1], padded[1:-1, 1:-1, 2:], padded[1:-1, 1:-1, :-2])


def face_terms(density, padded, scale):
    faces = tuple(scale * 2.0 / (density + other) for other in neighbour_slices(padded))
    total = faces[0] + faces[1] + faces[2] + faces[3] + faces[4] + faces[5]
    return faces, total


def apply_op(padded, field, faces, total):
    near = neighbour_slices(padded)
    beside = faces[0] * near[0] + faces[1] * near[1] + faces[2] * near[2]
    beside = beside + faces[3] * near[3] + faces[4] * near[4] + faces[5] * near[5]
    return total * field - beside


def sweep(field, level_rhs, faces, total):
    return field + omega_factor * (level_rhs - apply_op(jnp.pad(field, 1), field, faces, total)) / total


def coarsen(field):
    depth_x, depth_y, depth_z = field.shape
    return field.reshape(depth_x // 2, 2, depth_y // 2, 2, depth_z // 2, 2).mean(axis=(1, 3, 5))


def refine(field):
    depth_x, depth_y, depth_z = field.shape
    wide = jnp.broadcast_to(field[:, None, :, None, :, None], (depth_x, 2, depth_y, 2, depth_z, 2))
    return wide.reshape(2 * depth_x, 2 * depth_y, 2 * depth_z)


def reference(rhs, vof, disc_owner, disc_cell, disc_force):
    density = air_density + (1.0 - air_density) * (vof.astype(jnp.float32) / 1000.0)
    owner = disc_owner[:, :, 0]
    slab = jnp.arange(SLABS, dtype=jnp.int32)[:, None]
    pos_x = slab * CX + disc_cell // (CY * CZ)
    pos_y = owner * CY + (disc_cell // CZ) % CY
    pos_z = disc_cell % CZ
    source = jnp.zeros((NX, NY, CZ), jnp.float32).at[pos_x, pos_y, pos_z].add(disc_force)
    level_rhs = rhs + source
    operators = []
    for level in range(LEVELS + 1):
        if level > 0:
            density = coarsen(density)
        operators.append(face_terms(density, jnp.pad(density, 1), 0.25 ** level))
    stored = []
    for level in range(LEVELS):
        faces, total = operators[level]
        field = omega_factor * level_rhs / total
        for repeat in range(PRE - 1):
            field = sweep(field, level_rhs, faces, total)
        residual = level_rhs - apply_op(jnp.pad(field, 1), field, faces, total)
        stored.append((field, level_rhs))
        level_rhs = coarsen(residual)
    faces, total = operators[LEVELS]
    field = omega_factor * level_rhs / total
    for repeat in range(CSWEEPS - 1):
        field = sweep(field, level_rhs, faces, total)
    for level in range(LEVELS - 1, -1, -1):
        faces, total = operators[level]
        upper, upper_rhs = stored[level]
        field = upper + refine(field)
        for repeat in range(POST):
            field = sweep(field, upper_rhs, faces, total)
    return field
```

```python
import functools

import jax
import jax.numpy as jnp
from jax import lax
from jax.experimental import pallas as pl
from jax.experimental.pallas import tpu as pltpu
from jax.sharding import PartitionSpec as P

POST = 2
CSWEEPS = 8

air_density = 0.0012
omega_factor = 0.8

F32 = jnp.float32
BF16 = jnp.bfloat16
AXES = ("stream", "trans")

HALO = 12
HB = 10
HD = 11
NEAR = 8
FAR = 4
R0 = 4
ROWS0 = 48
R1 = 8
ROWS1 = 40
SHIFT1 = 10


def params(mib):
    return pltpu.CompilerParams(vmem_limit_bytes=mib << 20)


def lanes(shape):
    return lax.broadcasted_iota(jnp.int32, shape, len(shape) - 1)


def subs(shape):
    return lax.broadcasted_iota(jnp.int32, shape, len(shape) - 2)


def log2(n):
    assert n & (n - 1) == 0
    return n.bit_length() - 1


def up(x, st):
    return pltpu.roll(x, x.shape[-1] - st, x.ndim - 1)


def down(x, st):
    return pltpu.roll(x, st, x.ndim - 1)


def over(lo, hi, fn, limit=64, step=4):
    if hi - lo <= limit:
        for i in range(lo, hi):
            fn(i)
        return
    whole = (hi - lo) // step

    def chunk(k, carry):
        for j in range(step):
            fn(lo + k * step + j)
        return carry

    lax.fori_loop(0, whole, chunk, 0)
    for i in range(lo + whole * step, hi):
        fn(i)


def quotient(scale, den):
    return jnp.where(den > 0.0, scale / den, 0.0)


def setup(rho, faces, w, dg, x0, x1, r0, nr, st, level):
    cx, cy, cp = faces
    scale = 2.0 * 0.25**level
    nz = rho.shape[-1]
    rows = pl.ds(r0, nr)
    lane = lanes((nr, nz))
    first, last = lane < st, lane >= nz - st
    cx[x0 - 1, rows, :] = quotient(scale, rho[x0 - 1, rows, :] + rho[x0, rows, :])

    def plane(i):
        here = rho[i, rows, :]
        fx = quotient(scale, here + rho[i + 1, rows, :])
        cx[i, rows, :] = fx
        cy[i, rows, :] = quotient(scale, here + rho[i, pl.ds(r0 + 1, nr), :])
        fp = quotient(scale, here + jnp.where(last, 0.0, up(here, st)))
        fm = jnp.where(first, quotient(scale, here), down(fp, st))
        cp[i, rows, :] = jnp.where(last, 0.0, fp)
        diag = fx + cx[i - 1, rows, :] + cy[i, rows, :] + cy[i, pl.ds(r0 - 1, nr), :] + fp + fm
        dg[i, rows, :] = diag
        w[i, rows, :] = jnp.where(here > 0.0, omega_factor / diag, 0.0)

    over(x0, x1, plane)


def beside(v, faces, i, r0, nr, st):
    cx, cy, cp = faces
    rows = pl.ds(r0, nr)
    here = v[i, rows, :]
    total = cx[i, rows, :] * v[i + 1, rows, :] + cx[i - 1, rows, :] * v[i - 1, rows, :]
    total = total + cy[i, rows, :] * v[i, pl.ds(r0 + 1, nr), :]
    total = total + cy[i, pl.ds(r0 - 1, nr), :] * v[i, pl.ds(r0 - 1, nr), :]
    fz = cp[i, rows, :]
    total = total + (fz * up(here, st) + down(fz * here, st))
    return here, total


def start(v, b, w, x0, x1, r0, nr):
    rows = pl.ds(r0, nr)

    def plane(i):
        v[i, rows, :] = w[i, rows, :] * b[i, rows, :]

    over(x0, x1, plane)


def swept(v, b, w, faces, i, r0, nr, st):
    rows = pl.ds(r0, nr)
    here, total = beside(v, faces, i, r0, nr, st)
    return (1.0 - omega_factor) * here + w[i, rows, :] * (b[i, rows, :] + total)


def sweep(v, out, b, w, faces, x0, x1, r0, nr, st):
    def plane(i):
        out[i, pl.ds(r0, nr), :] = swept(v, b, w, faces, i, r0, nr, st)

    over(x0, x1, plane)


def residual(v, b, dg, faces, i, r0, nr, st):
    here, total = beside(v, faces, i, r0, nr, st)
    rows = pl.ds(r0, nr)
    return b[i, rows, :] + (total - dg[i, rows, :] * here)


def coarsen(fine, out, tmp, pairs, r0, nr, st, to):
    def pair(a, c):
        total = fine(a) + fine(a + 1)
        even = (lanes(total.shape) // st) % 2 == 0
        total = total + jnp.where(even, up(total, st), down(total, st))
        tmp[c, pl.ds(0, nr), :] = total
        half = nr // 2
        out[c, pl.ds(to, half), :] = 0.125 * (
            tmp[c, pl.ds(0, half, stride=2), :] + tmp[c, pl.ds(1, half, stride=2), :]
        )

    a0, c0, count = pairs
    over(0, count, lambda k: pair(a0 + 2 * k, c0 + k))


def doubled(ref, k, row, value):
    n = value.shape[0]
    ref[k, pl.ds(row, n, stride=2), :] = value
    ref[k, pl.ds(row + 1, n, stride=2), :] = value


def half_tile(a, b, upper):
    top = subs(a.shape) < FAR
    return jnp.where(
        upper,
        jnp.where(top, pltpu.roll(a, FAR, 0), b),
        jnp.where(top, a, pltpu.roll(b, FAR, 0)),
    )


def pack_kernel(groups, rhs, vof, owner, cell, force, dens, xa, xb, ya, yb, disc):
    nx, ny, nz = rhs.shape
    s_even = lax.axis_index("stream") % 2 == 0
    t_even = lax.axis_index("trans") % 2 == 0
    for i in range(nx):
        dens[i] = air_density + ((1.0 - air_density) / 1000.0) * vof[i].astype(F32)
    tail_b, tail_d = nx - HB, nx - HD
    for out, tail in ((xa, s_even), (xb, jnp.logical_not(s_even))):
        at_b, at_d = jnp.where(tail, tail_b, 0), jnp.where(tail, tail_d, 0)
        for i in range(HB):
            out[i] = rhs[at_b + i]
        for i in range(HD):
            out[HB + i] = dens[at_d + i]
    for i in range(nx):
        b, d = rhs[i], dens[i]
        mid_b, mid_d = b[FAR : FAR + 8], d[FAR : FAR + 8]
        for out, tail in ((ya, t_even), (yb, jnp.logical_not(t_even))):
            out[i] = jnp.where(tail, b[ny - NEAR :], b[:NEAR])
            out[nx + i] = jnp.where(tail, d[ny - NEAR :], d[:NEAR])
            out[2 * nx + i] = half_tile(mid_b, mid_d, jnp.logical_not(tail))
    key = (owner[...] * (nx * ny * nz) + cell[...]).astype(F32)
    rows = key.shape[0]
    values = jnp.concatenate([key, force[...]], axis=0)
    if 2 * rows < 8:
        values = jnp.concatenate([values] * (4 // rows), axis=0)
    for g in range(groups * 2 * rows // 8):
        disc[pl.ds(8 * g, 8), :] = values


def corner_kernel(xa, xb, ca, cb):
    ny = xa.shape[1]
    s_even = lax.axis_index("stream") % 2 == 0
    t_even = lax.axis_index("trans") % 2 == 0
    base = 0
    for x, high in ((xa, s_even), (xb, jnp.logical_not(s_even))):
        for i in range(HB + HD):
            tile = x[i]
            low_rows, high_rows = tile[:NEAR], tile[ny - NEAR :]
            ca[base + i] = jnp.where(t_even, high_rows, low_rows)
            cb[base + i] = jnp.where(t_even, low_rows, high_rows)
        at_b = jnp.where(high, 0, HB - FAR)
        at_d = jnp.where(high, HB, HB + HD - FAR)
        for i in range(FAR):
            mid_b = x[at_b + i, pl.ds(FAR, 8), :]
            mid_d = x[at_d + i, pl.ds(FAR, 8), :]
            ca[base + HB + HD + i] = half_tile(mid_b, mid_d, jnp.logical_not(t_even))
            cb[base + HB + HD + i] = half_tile(mid_b, mid_d, t_even)
        base += HB + HD + FAR


def source_kernel(shape, disc, out, hot, val):
    nx, ny, nz = shape
    slabs, groups = lax.axis_size("stream"), lax.axis_size("trans")
    s, t = lax.axis_index("stream"), lax.axis_index("trans")
    per_slab = disc.shape[0] // slabs
    part = per_slab // groups // 2
    wide = ny + 2 * HALO
    depth = lanes((8, nz))[:1]
    for where_, first_x, count, to in ((-1, nx - HB, HB, 0), (0, 0, nx, HB), (1, 0, HB, HB + nx)):
        slab = s + where_

        def fill(slab=slab, first_x=first_x, count=count, to=to):
            base = pl.multiple_of(slab * per_slab, 8)
            cols = part * groups * nz
            zrow = subs((nz, nz))
            mrow = subs((count * wide, nz))
            for g in range(groups):
                for p in range(part):
                    at = (g * part + p) * nz
                    tile = disc[pl.ds(base + (g * 2 * part) // 8 * 8, 8), :]
                    r = (g * 2 * part) % 8 + p
                    key = tile[r : r + 1].astype(jnp.int32)
                    f = tile[r + part : r + part + 1]
                    z = key & (nz - 1)
                    y = (key >> log2(nz)) & (ny - 1)
                    x = (key >> log2(nz * ny)) & (nx - 1)
                    o = key >> log2(nz * ny * nx)
                    row = (o - t) * ny + y + HALO
                    ok = (row >= 0) & (row < wide) & (x >= first_x) & (x < first_x + count)
                    m = jnp.where(ok, (x - first_x) * wide + row, -1)
                    hot[pl.ds(0, count * wide), pl.ds(at, nz)] = (
                        jnp.where(mrow == m, 1.0, 0.0).astype(BF16)
                    )
                    hi = f.astype(BF16).astype(F32)
                    mid = (f - hi).astype(BF16).astype(F32)
                    low = f - hi - mid
                    here = zrow == z
                    for q, piece in enumerate((hi, mid, low)):
                        val[pl.ds(q * nz, nz), pl.ds(at, nz)] = (
                            jnp.where(here, piece, 0.0).astype(BF16)
                        )
            got = lax.dot_general(
                hot[pl.ds(0, count * wide), pl.ds(0, cols)],
                val[:, pl.ds(0, cols)],
                (((1,), (1,)), ((), ())),
                preferred_element_type=F32,
            )
            got = got[:, :nz] + got[:, nz : 2 * nz] + got[:, 2 * nz :]
            for i in range(count):
                out[to + i] = got[i * wide : (i + 1) * wide]

        if where_ == 0:
            fill()
        else:
            inside = slab >= 0 if where_ < 0 else slab < slabs
            pl.when(inside)(fill)

            @pl.when(jnp.logical_not(inside))
            def _(count=count, to=to):
                for i in range(count):
                    out[to + i] = jnp.zeros(out.shape[1:], F32)


def pre_kernel(
    rhs, dens, xa, xb, ya, yb, ca, cb, source,
    slots, v0, b0, w0, cx0, cy0, cp0, v1, b1, w1, cx1, cy1, cp1,
    rho0, dg0, u0, rho1, dg1, u1, tmp0, tmp1,
):
    nx, ny, nz = rhs.shape
    s, t = lax.axis_index("stream"), lax.axis_index("trans")
    groups = lax.axis_size("trans")
    s_even, t_even = s % 2 == 0, t % 2 == 0
    own = R0 + HALO
    full = nx + 2 * HALO
    zero0 = jnp.zeros((ROWS0, nz), F32)
    for i in range(full):
        rho0[i] = zero0
        b0[i] = zero0
    for i in range(nx):
        b0[HALO + i, pl.ds(own, ny), :] = rhs[i]
        rho0[HALO + i, pl.ds(own, ny), :] = dens[i]

    def sides(a, b):
        low = jnp.where(t_even, b, a)
        high = jnp.where(t_even, a, b)
        return jnp.where(t > 0, low, 0.0), jnp.where(t < groups - 1, high, 0.0)

    def near(ref, i, a, b):
        low, high = sides(a, b)
        ref[i, pl.ds(own - NEAR, NEAR), :] = low
        ref[i, pl.ds(own + ny, NEAR), :] = high

    def far(i, a, b):
        low, high = sides(a, b)
        b0[i, pl.ds(own - NEAR - FAR, FAR), :] = low[:FAR]
        b0[i, pl.ds(own + ny + NEAR, FAR), :] = high[:FAR]
        rho0[i, pl.ds(own - NEAR - FAR, FAR), :] = low[FAR:]
        rho0[i, pl.ds(own + ny + NEAR, FAR), :] = high[FAR:]

    for i in range(nx):
        near(b0, HALO + i, ya[i], yb[i])
        near(rho0, HALO + i, ya[nx + i], yb[nx + i])
        far(HALO + i, ya[2 * nx + i], yb[2 * nx + i])
    base = 0
    for x, high in ((xa, s_even), (xb, jnp.logical_not(s_even))):
        at_b = jnp.where(high, HALO + nx, HALO - HB)
        at_d = jnp.where(high, HALO + nx, HALO - HD)
        at_f = jnp.where(high, HALO + nx, HALO - FAR)
        for i in range(HB):
            b0[at_b + i, pl.ds(own, ny), :] = x[i]
            near(b0, at_b + i, ca[base + i], cb[base + i])
        for i in range(HD):
            rho0[at_d + i, pl.ds(own, ny), :] = x[HB + i]
            near(rho0, at_d + i, ca[base + HB + i], cb[base + HB + i])
        for i in range(FAR):
            k = base + HB + HD + i
            far(at_f + i, ca[k], cb[k])
        base += HB + HD + FAR
    wide = ny + 2 * HALO
    for i in range(nx + 2 * HB):
        at = HALO - HB + i
        b0[at, pl.ds(R0, wide), :] = b0[at, pl.ds(R0, wide), :] + source[i]

    f0 = (cx0, cy0, cp0)
    lo, hi = HALO - HB, HALO + nx + HB
    zero_row = jnp.zeros((1, nz), F32)
    for i in range(lo - 1, hi + 1):
        for ref in (u0, v0, cy0):
            ref[i, pl.ds(R0 - 1, 1), :] = zero_row
        for ref in (u0, v0):
            ref[i, pl.ds(R0 + wide, 1), :] = zero_row
    setup(rho0, f0, w0, dg0, lo, hi, R0, wide, 1, 0)
    start(u0, b0, w0, lo, hi, R0, wide)
    sweep(u0, v0, b0, w0, f0, lo + 1, hi - 1, R0, wide, 1)

    half = nx // 2 + HALO
    wide1 = 24
    zero1 = jnp.zeros((ROWS1, nz), F32)
    for i in range(half):
        for ref in (rho1, b1, u1, v1, cy1):
            ref[i] = zero1
    for i in range(half):
        tmp0[i] = zero0

    def rho_rows(i):
        return rho0[i, pl.ds(R0, wide), :]

    rows_to = SHIFT1
    coarsen(rho_rows, rho1, tmp0, (2, 1, half - 2), R0, wide, 1, rows_to)

    def res_rows(i):
        return residual(v0, b0, dg0, f0, i, R0, wide, 1)

    coarsen(res_rows, b1, tmp0, (lo + 2, (lo + 2) // 2, (hi - lo - 4) // 2), R0, wide, 1, rows_to)
    f1 = (cx1, cy1, cp1)
    lo1, hi1 = (lo + 2) // 2, (hi - 2) // 2
    setup(rho1, f1, w1, dg1, lo1, hi1, R1, wide1, 2, 1)
    start(u1, b1, w1, lo1, hi1, R1, wide1)
    sweep(u1, v1, b1, w1, f1, lo1 + 1, hi1 - 1, R1, wide1, 2)

    own1 = SHIFT1 + HALO // 2
    ny1 = ny // 2
    first1 = HALO // 2

    def packed(fine):
        total = None
        for k in range(nx // 4):
            a = first1 + 2 * k
            pairs = fine(a) + fine(a + 1)
            even = (lanes(pairs.shape) // 2) % 2 == 0
            pairs = pairs + jnp.where(even, up(pairs, 2), down(pairs, 2))
            turn = lanes(pairs.shape) % 4 == k
            total = jnp.where(turn, pairs, 0.0 if total is None else total)
        tmp1[...] = total
        return 0.125 * (tmp1[pl.ds(0, ny1 // 2, stride=2), :] + tmp1[pl.ds(1, ny1 // 2, stride=2), :])

    rows2 = ny1 // 2
    slots[0, pl.ds(0, rows2), :] = packed(
        lambda i: residual(v1, b1, dg1, f1, i, own1, ny1, 2)
    )
    slots[0, pl.ds(rows2, rows2), :] = packed(lambda i: rho1[i, pl.ds(own1, ny1), :])
    slot = slots[0]

    def put(g):
        slots[g] = slot

    over(1, slots.shape[0], put)


class Coarse:
    def __init__(self, k, refs, planes, rows, mult, nz):
        self.rho, self.cx, self.cy, self.cp, self.w, self.dg, self.b, self.va, self.vb = refs
        self.planes, self.rows = planes, rows
        self.pitch, self.mult, self.st = 1 << k, mult >> k, mult << k
        self.level = 2 + k
        lane = lanes((rows, nz))
        self.sub = (lane // self.pitch) % self.mult
        self.even_z = (lane // self.st) % 2 == 0
        self.first, self.last = lane < self.st, lane >= nz - self.st
        self.at = pl.ds(8, rows)

    def each(self, fn):
        over(1, 1 + self.planes, fn, 8, 2)

    def next_x(self, here, above):
        if self.mult == 1:
            return above
        far = down(above, (self.mult - 1) * self.pitch)
        return jnp.where(self.sub == self.mult - 1, far, up(here, self.pitch))

    def prev_x(self, here, below):
        if self.mult == 1:
            return below
        far = up(below, (self.mult - 1) * self.pitch)
        return jnp.where(self.sub == 0, far, down(here, self.pitch))

    def setup(self):
        scale = 2.0 * 0.25**self.level
        rho, cx, cy, cp, at, n = self.rho, self.cx, self.cy, self.cp, self.at, self.rows
        cx[0, at, :] = quotient(scale, self.next_x(rho[0, at, :], rho[1, at, :]))

        def plane(i):
            here = rho[i, at, :]
            fx = quotient(scale, here + self.next_x(here, rho[i + 1, at, :]))
            cx[i, at, :] = fx
            cy[i, pl.ds(0, n + 8), :] = quotient(
                scale, rho[i, pl.ds(0, n + 8), :] + rho[i, pl.ds(1, n + 8), :]
            )
            fp = quotient(scale, here + jnp.where(self.last, 0.0, up(here, self.st)))
            fm = jnp.where(self.first, quotient(scale, here), down(fp, self.st))
            cp[i, at, :] = jnp.where(self.last, 0.0, fp)
            diag = fx + self.prev_x(fx, cx[i - 1, at, :]) + fp + fm
            diag = diag + cy[i, at, :] + cy[i, pl.ds(7, n), :]
            self.dg[i, at, :] = diag
            self.w[i, at, :] = omega_factor / diag

        self.each(plane)

    def beside(self, v, i):
        at, n = self.at, self.rows
        here = v[i, at, :]
        fx, fz = self.cx[i, at, :], self.cp[i, at, :]
        total = fx * self.next_x(here, v[i + 1, at, :])
        total = total + self.prev_x(fx * here, self.cx[i - 1, at, :] * v[i - 1, at, :])
        total = total + self.cy[i, at, :] * v[i, pl.ds(9, n), :]
        total = total + self.cy[i, pl.ds(7, n), :] * v[i, pl.ds(7, n), :]
        return here, total + (fz * up(here, self.st) + down(fz * here, self.st))

    def start(self):
        def plane(i):
            self.va[i, self.at, :] = self.w[i, self.at, :] * self.b[i, self.at, :]

        self.each(plane)

    def smooth(self, n):
        for _ in range(n):

            def plane(i):
                here, total = self.beside(self.va, i)
                self.vb[i, self.at, :] = (1.0 - omega_factor) * here + self.w[i, self.at, :] * (
                    self.b[i, self.at, :] + total
                )

            self.each(plane)
            self.va, self.vb = self.vb, self.va

    def residual(self, i):
        here, total = self.beside(self.va, i)
        return self.b[i, self.at, :] + (total - self.dg[i, self.at, :] * here)

    def coarsen(self, fine, out, tmp):
        def plane(i):
            total = fine(i)
            even_x = self.sub % 2 == 0
            total = total + jnp.where(even_x, up(total, self.pitch), down(total, self.pitch))
            total = total + jnp.where(self.even_z, up(total, self.st), down(total, self.st))
            tmp[i, pl.ds(0, self.rows), :] = total
            half = self.rows // 2
            out[i, pl.ds(8, half), :] = 0.125 * (
                tmp[i, pl.ds(0, half, stride=2), :] + tmp[i, pl.ds(1, half, stride=2), :]
            )

        self.each(plane)

    def correct(self, below, tmp):
        def plane(i):
            doubled(tmp, i, 0, below.va[i, below.at, :])
            self.va[i, self.at, :] = self.va[i, self.at, :] + tmp[i, pl.ds(0, self.rows), :]

        self.each(plane)


def post_kernel(slots, v0, b0, w0, cx0, cy0, cp0, v1, b1, w1, cx1, cy1, cp1, out, *refs):
    nx, ny, nz = out.shape
    slabs, groups = lax.axis_size("stream"), lax.axis_size("trans")
    s, t = lax.axis_index("stream"), lax.axis_index("trans")
    gx, gy = nx // 4, ny // 4
    assert gx * (nz // 4) == nz
    rows = groups * gy
    levels = [Coarse(k, refs[9 * k : 9 * k + 9], slabs, rows >> k, gx, nz) for k in range(3)]
    tmp, e1, u1, x1, e0, u0, x0 = refs[27:]
    for c in levels:
        zero = jnp.zeros((c.rows + 16, nz), F32)

        def clear(i, group=(c.rho, c.va, c.vb), zero=zero):
            for ref in group:
                ref[i] = zero

        over(0, slabs + 2, clear)

    two, three, four = levels
    top = subs((8, nz)) < 4

    def unpack(sl):
        for pair in range(groups // 2):
            first = slots[sl * groups + 2 * pair]
            second = slots[sl * groups + 2 * pair + 1]
            to = pl.ds(8 + 8 * pair, 8)
            two.b[1 + sl, to, :] = jnp.where(top, first, pltpu.roll(second, 4, 0))
            two.rho[1 + sl, to, :] = jnp.where(top, pltpu.roll(first, 4, 0), second)

    over(0, slabs, unpack, 8, 2)
    two.setup()
    two.coarsen(lambda i: two.rho[i, two.at, :], three.rho, tmp)
    three.setup()
    three.coarsen(lambda i: three.rho[i, three.at, :], four.rho, tmp)
    four.setup()
    two.start()
    two.smooth(1)
    two.coarsen(two.residual, three.b, tmp)
    three.start()
    three.smooth(1)
    three.coarsen(three.residual, four.b, tmp)
    four.start()
    four.smooth(CSWEEPS - 1)
    three.correct(four, tmp)
    three.smooth(POST)
    two.correct(three, tmp)
    two.smooth(POST)

    f1 = (cx1, cy1, cp1)
    first1, nx1 = HALO // 2, nx // 2
    wide1 = 24
    for i in range(e1.shape[0]):
        e1[i] = jnp.zeros((ROWS1, nz), F32)
    zero_row = jnp.zeros((1, nz), F32)
    for i in range(u1.shape[0]):
        for ref in (u1, x1):
            ref[i, pl.ds(R1 - 1, 1), :] = zero_row
            ref[i, pl.ds(R1 + wide1, 1), :] = zero_row
    place = lanes((gy + 4, nz)) % gx
    around = [two.va[s + k, pl.ds(t * gy + 6, gy + 4), :] for k in range(3)]
    for k in range(gx + 4):
        plane, sub = around[(k + gx - 2) // gx], (k + gx - 2) % gx
        value = plane if sub == 0 else pltpu.roll(plane, nz - sub, 1)
        for m in range(1, gx):
            value = jnp.where(place == m, pltpu.roll(plane, (m - sub) % nz, 1) if m != sub else plane, value)
        doubled(e1, k, SHIFT1 + first1 - 4, value)
    rows1 = pl.ds(R1, wide1)
    for i in range(first1 - 3, first1 + nx1 + 3):
        u1[i, rows1, :] = v1[i, rows1, :] + e1[(i - first1 + 4) // 2, rows1, :]
    sweep(u1, x1, b1, w1, f1, first1 - 2, first1 + nx1 + 2, R1, wide1, 2)
    sweep(x1, u1, b1, w1, f1, first1 - 1, first1 + nx1 + 1, R1, wide1, 2)

    f0 = (cx0, cy0, cp0)
    own = R0 + HALO
    low, count = own - 8, ny + 16
    for k in range(nx1 + 2):
        value = u1[first1 - 1 + k, pl.ds(SHIFT1 + first1 - 4, ny // 2 + 8), :]
        doubled(e0, k, low, value)
    for i in range(HALO - 2, HALO + nx + 2):
        rows0 = pl.ds(low, count)
        u0[i, rows0, :] = v0[i, rows0, :] + e0[(i - HALO + 2) // 2, rows0, :]
    sweep(u0, x0, b0, w0, f0, HALO - 1, HALO + nx + 1, low + 7, count - 8, 1)
    for i in range(nx):
        out[i] = swept(x0, b0, w0, f0, HALO + i, own, ny, 1)


def exchange(count, other, parity, open_ends):
    pairs = []
    for i in range(count):
        j = ((i + parity) ^ 1) - parity
        if 0 <= j < count:
            pairs.append((i, j))
        elif not open_ends:
            pairs.append((i, count - 1 - i))
    return pairs


def swap(value, axis, parity, open_ends):
    count = lax.axis_size(axis)
    return lax.ppermute(value, axis, exchange(count, None, parity, open_ends))


def sds(*shape):
    return jax.ShapeDtypeStruct(shape, F32)


def body(rhs, vof, disc_owner, disc_cell, disc_force):
    nx, ny, nz = rhs.shape
    slabs, groups = lax.axis_size("stream"), lax.axis_size("trans")
    devices = slabs * groups
    rows = disc_cell.shape[1] // nz
    wide = ny + 2 * HALO
    halo_x = sds(HB + HD, ny, nz)
    halo_y = sds(3 * nx, 8, nz)
    corner = sds(2 * (HB + HD + FAR), 8, nz)

    dens, xa, xb, ya, yb, disc = pl.pallas_call(
        functools.partial(pack_kernel, devices),
        out_shape=(sds(nx, ny, nz), halo_x, halo_x, halo_y, halo_y, sds(devices * 2 * rows, nz)),
        compiler_params=params(12),
        name="pack",
    )(
        rhs,
        vof,
        disc_owner.reshape(rows, nz),
        disc_cell.reshape(rows, nz),
        disc_force.reshape(rows, nz),
    )
    disc = lax.all_to_all(disc, AXES, 0, 0, tiled=True)
    xa = swap(xa, "stream", 0, True)
    xb = swap(xb, "stream", 1, True)
    ya = swap(ya, "trans", 0, False)
    yb = swap(yb, "trans", 1, False)
    ca, cb = pl.pallas_call(
        corner_kernel, out_shape=(corner, corner), compiler_params=params(8), name="corner"
    )(xa, xb)
    ca = swap(ca, "trans", 0, False)
    cb = swap(cb, "trans", 1, False)
    cols = groups * rows * nz
    source = pl.pallas_call(
        functools.partial(source_kernel, (nx, ny, nz)),
        out_shape=sds(nx + 2 * HB, wide, nz),
        scratch_shapes=[pltpu.VMEM((nx * wide, cols), BF16), pltpu.VMEM((3 * nz, cols), BF16)],
        compiler_params=params(24),
        name="source",
    )(disc)
    full, half = nx + 2 * HALO, nx // 2 + HALO
    frame0, frame1 = sds(full, ROWS0, nz), sds(half, ROWS1, nz)
    s0, s1 = pltpu.VMEM(frame0.shape, F32), pltpu.VMEM(frame1.shape, F32)
    slots, *state = pl.pallas_call(
        pre_kernel,
        out_shape=(sds(devices, 8, nz), *([frame0] * 6), *([frame1] * 6)),
        scratch_shapes=[
            s0, s0, s0, s1, s1, s1,
            pltpu.VMEM((half, ROWS0, nz), F32), pltpu.VMEM((ny // 2, nz), F32),
        ],
        compiler_params=params(28),
        name="presmooth",
    )(rhs, dens, xa, xb, ya, yb, ca, cb, source)
    slots = lax.all_to_all(slots, AXES, 0, 0, tiled=True)
    gy = groups * ny // 4
    scratch = [pltpu.VMEM((slabs + 2, (gy >> k) + 16, nz), F32) for k in range(3) for _ in range(9)]
    scratch += [
        pltpu.VMEM((slabs + 2, gy, nz), F32),
        pltpu.VMEM((nx // 4 + 4, ROWS1, nz), F32),
        s1,
        s1,
        pltpu.VMEM((nx // 2 + 2, ROWS0, nz), F32),
        s0,
        s0,
    ]
    return pl.pallas_call(
        post_kernel,
        out_shape=sds(nx, ny, nz),
        scratch_shapes=scratch,
        compiler_params=params(28),
        name="postsmooth",
    )(slots, *state)


def solution(mesh):
    return jax.shard_map(
        body,
        mesh=mesh,
        in_specs=(
            P("stream", "trans", None),
            P("stream", "trans", None),
            P("stream", "trans", None),
            P("stream", "trans"),
            P("stream", "trans"),
        ),
        out_specs=P("stream", "trans", None),
        check_vma=False,
    )
```

```python
import functools

import jax
import jax.numpy as jnp
from jax import lax
from jax.experimental import pallas as pl
from jax.experimental.pallas import tpu as pltpu
from jax.sharding import PartitionSpec as P


POST = 2
CSWEEPS = 8

air_density = 0.0012
omega_factor = 0.8

F32 = jnp.float32
BF16 = jnp.bfloat16
AXES = ("stream", "trans")

HALO = 12
HB = 10
HD = 11
NEAR = 8
FAR = 4
R0 = 4
ROWS0 = 48
R1 = 8
ROWS1 = 40
SHIFT1 = 10


def params(mib):
    return pltpu.CompilerParams(vmem_limit_bytes=mib << 20)


def lanes(shape):
    return lax.broadcasted_iota(jnp.int32, shape, len(shape) - 1)


def subs(shape):
    return lax.broadcasted_iota(jnp.int32, shape, len(shape) - 2)


def log2(n):
    assert n & (n - 1) == 0
    return n.bit_length() - 1


def up(x, st):
    return pltpu.roll(x, x.shape[-1] - st, x.ndim - 1)


def down(x, st):
    return pltpu.roll(x, st, x.ndim - 1)


def over(lo, hi, fn, limit=64, step=4):
    if hi - lo <= limit:
        for i in range(lo, hi):
            fn(i)
        return
    whole = (hi - lo) // step

    def chunk(k, carry):
        for j in range(step):
            fn(lo + k * step + j)
        return carry

    lax.fori_loop(0, whole, chunk, 0)
    for i in range(lo + whole * step, hi):
        fn(i)


def quotient(scale, den):
    return jnp.where(den > 0.0, scale / den, 0.0)


def setup(rho, faces, w, dg, x0, x1, r0, nr, st, level):
    cx, cy, cp = faces
    scale = 2.0 * 0.25**level
    nz = rho.shape[-1]
    rows = pl.ds(r0, nr)
    lane = lanes((nr, nz))
    first, last = lane < st, lane >= nz - st
    cx[x0 - 1, rows, :] = quotient(scale, rho[x0 - 1, rows, :] + rho[x0, rows, :])

    def plane(i):
        here = rho[i, rows, :]
        fx = quotient(scale, here + rho[i + 1, rows, :])
        cx[i, rows, :] = fx
        cy[i, rows, :] = quotient(scale, here + rho[i, pl.ds(r0 + 1, nr), :])
        fp = quotient(scale, here + jnp.where(last, 0.0, up(here, st)))
        fm = jnp.where(first, quotient(scale, here), down(fp, st))
        cp[i, rows, :] = jnp.where(last, 0.0, fp)
        diag = fx + cx[i - 1, rows, :] + cy[i, rows, :] + cy[i, pl.ds(r0 - 1, nr), :] + fp + fm
        dg[i, rows, :] = diag
        w[i, rows, :] = jnp.where(here > 0.0, omega_factor / diag, 0.0)

    over(x0, x1, plane)


def beside(v, faces, i, r0, nr, st):
    cx, cy, cp = faces
    rows = pl.ds(r0, nr)
    here = v[i, rows, :]
    total = cx[i, rows, :] * v[i + 1, rows, :] + cx[i - 1, rows, :] * v[i - 1, rows, :]
    total = total + cy[i, rows, :] * v[i, pl.ds(r0 + 1, nr), :]
    total = total + cy[i, pl.ds(r0 - 1, nr), :] * v[i, pl.ds(r0 - 1, nr), :]
    fz = cp[i, rows, :]
    total = total + (fz * up(here, st) + down(fz * here, st))
    return here, total


def start(v, b, w, x0, x1, r0, nr):
    rows = pl.ds(r0, nr)

    def plane(i):
        v[i, rows, :] = w[i, rows, :] * b[i, rows, :]

    over(x0, x1, plane)


def swept(v, b, w, faces, i, r0, nr, st):
    rows = pl.ds(r0, nr)
    here, total = beside(v, faces, i, r0, nr, st)
    return (1.0 - omega_factor) * here + w[i, rows, :] * (b[i, rows, :] + total)


def sweep(v, out, b, w, faces, x0, x1, r0, nr, st):
    def plane(i):
        out[i, pl.ds(r0, nr), :] = swept(v, b, w, faces, i, r0, nr, st)

    over(x0, x1, plane)


def residual(v, b, dg, faces, i, r0, nr, st):
    here, total = beside(v, faces, i, r0, nr, st)
    rows = pl.ds(r0, nr)
    return b[i, rows, :] + (total - dg[i, rows, :] * here)


def coarsen(fine, out, tmp, pairs, nr, st, to):
    def pair(a, c):
        total = fine(a) + fine(a + 1)
        even = (lanes(total.shape) // st) % 2 == 0
        total = total + jnp.where(even, up(total, st), down(total, st))
        tmp[c, pl.ds(0, nr), :] = total
        half = nr // 2
        out[c, pl.ds(to, half), :] = 0.125 * (
            tmp[c, pl.ds(0, half, stride=2), :] + tmp[c, pl.ds(1, half, stride=2), :]
        )

    a0, c0, count = pairs
    over(0, count, lambda k: pair(a0 + 2 * k, c0 + k))


def doubled(ref, k, row, value):
    n = value.shape[0]
    ref[k, pl.ds(row, n, stride=2), :] = value
    ref[k, pl.ds(row + 1, n, stride=2), :] = value


def half_tile(a, b, upper):
    top = subs(a.shape) < FAR
    return jnp.where(
        upper,
        jnp.where(top, pltpu.roll(a, FAR, 0), b),
        jnp.where(top, a, pltpu.roll(b, FAR, 0)),
    )


def pack_kernel(groups, *refs):
    outside, (rhs, dens, xa, xb, ya, yb, disc) = refs[:5], refs[5:12]
    vof, owner, cell, force, sems = refs[12:]
    inside = (rhs, vof, owner, cell, force)
    copies = [
        pltpu.make_async_copy(a, b, sems.at[i]) for i, (a, b) in enumerate(zip(outside, inside))
    ]
    for copy in copies:
        copy.start()
    for copy in copies:
        copy.wait()
    nx, ny, nz = rhs.shape
    s_even = lax.axis_index("stream") % 2 == 0
    t_even = lax.axis_index("trans") % 2 == 0
    for i in range(nx):
        dens[i] = air_density + ((1.0 - air_density) / 1000.0) * vof[i].astype(F32)
    tail_b, tail_d = nx - HB, nx - HD
    for out, tail in ((xa, s_even), (xb, jnp.logical_not(s_even))):
        at_b, at_d = jnp.where(tail, tail_b, 0), jnp.where(tail, tail_d, 0)
        for i in range(HB):
            out[i] = rhs[at_b + i]
        for i in range(HD):
            out[HB + i] = dens[at_d + i]
    for i in range(nx):
        b, d = rhs[i], dens[i]
        mid_b, mid_d = b[FAR : FAR + 8], d[FAR : FAR + 8]
        for out, tail in ((ya, t_even), (yb, jnp.logical_not(t_even))):
            out[i] = jnp.where(tail, b[ny - NEAR :], b[:NEAR])
            out[nx + i] = jnp.where(tail, d[ny - NEAR :], d[:NEAR])
            out[2 * nx + i] = half_tile(mid_b, mid_d, jnp.logical_not(tail))
    key = (owner[...] * (nx * ny * nz) + cell[...]).astype(F32)
    rows = key.shape[0]
    values = jnp.concatenate([key, force[...]], axis=0)
    if 2 * rows < 8:
        values = jnp.concatenate([values] * (4 // rows), axis=0)
    for g in range(groups * 2 * rows // 8):
        disc[pl.ds(8 * g, 8), :] = values


def corner_kernel(xa, xb, ca, cb):
    ny = xa.shape[1]
    s_even = lax.axis_index("stream") % 2 == 0
    t_even = lax.axis_index("trans") % 2 == 0
    base = 0
    for x, high in ((xa, s_even), (xb, jnp.logical_not(s_even))):
        for i in range(HB + HD):
            tile = x[i]
            low_rows, high_rows = tile[:NEAR], tile[ny - NEAR :]
            ca[base + i] = jnp.where(t_even, high_rows, low_rows)
            cb[base + i] = jnp.where(t_even, low_rows, high_rows)
        at_b = jnp.where(high, 0, HB - FAR)
        at_d = jnp.where(high, HB, HB + HD - FAR)
        for i in range(FAR):
            mid_b = x[at_b + i, pl.ds(FAR, 8), :]
            mid_d = x[at_d + i, pl.ds(FAR, 8), :]
            ca[base + HB + HD + i] = half_tile(mid_b, mid_d, jnp.logical_not(t_even))
            cb[base + HB + HD + i] = half_tile(mid_b, mid_d, t_even)
        base += HB + HD + FAR


def source_kernel(shape, disc, out, hot, val):
    nx, ny, nz = shape
    slabs, groups = lax.axis_size("stream"), lax.axis_size("trans")
    s, t = lax.axis_index("stream"), lax.axis_index("trans")
    per_slab = disc.shape[0] // slabs
    part = per_slab // groups // 2
    wide = ny + 2 * HALO
    depth = lanes((8, nz))[:1]
    for where_, first_x, count, to in ((-1, nx - HB, HB, 0), (0, 0, nx, HB), (1, 0, HB, HB + nx)):
        slab = s + where_

        def fill(slab=slab, first_x=first_x, count=count, to=to):
            base = pl.multiple_of(slab * per_slab, 8)
            cols = part * groups * nz
            zrow = subs((nz, nz))
            mrow = subs((count * wide, nz))
            for g in range(groups):
                for p in range(part):
                    at = (g * part + p) * nz
                    tile = disc[pl.ds(base + (g * 2 * part) // 8 * 8, 8), :]
                    r = (g * 2 * part) % 8 + p
                    key = tile[r : r + 1].astype(jnp.int32)
                    f = tile[r + part : r + part + 1]
                    z = key & (nz - 1)
                    y = (key >> log2(nz)) & (ny - 1)
                    x = (key >> log2(nz * ny)) & (nx - 1)
                    o = key >> log2(nz * ny * nx)
                    row = (o - t) * ny + y + HALO
                    ok = (row >= 0) & (row < wide) & (x >= first_x) & (x < first_x + count)
                    m = jnp.where(ok, (x - first_x) * wide + row, -1)
                    hot[pl.ds(0, count * wide), pl.ds(at, nz)] = (
                        jnp.where(mrow == m, 1.0, 0.0).astype(BF16)
                    )
                    hi = f.astype(BF16).astype(F32)
                    mid = (f - hi).astype(BF16).astype(F32)
                    low = f - hi - mid
                    here = zrow == z
                    for q, piece in enumerate((hi, mid, low)):
                        val[pl.ds(q * nz, nz), pl.ds(at, nz)] = (
                            jnp.where(here, piece, 0.0).astype(BF16)
                        )
            got = lax.dot_general(
                hot[pl.ds(0, count * wide), pl.ds(0, cols)],
                val[:, pl.ds(0, cols)],
                (((1,), (1,)), ((), ())),
                preferred_element_type=F32,
            )
            got = got[:, :nz] + got[:, nz : 2 * nz] + got[:, 2 * nz :]
            for i in range(count):
                out[to + i] = got[i * wide : (i + 1) * wide]

        if where_ == 0:
            fill()
        else:
            inside = slab >= 0 if where_ < 0 else slab < slabs
            pl.when(inside)(fill)

            @pl.when(jnp.logical_not(inside))
            def _(count=count, to=to):
                for i in range(count):
                    out[to + i] = jnp.zeros(out.shape[1:], F32)


def pre_kernel(
    rhs, dens, xa, xb, ya, yb, ca, cb, source,
    slots, v0, b0, w0, cx0, cy0, cp0, v1, b1, w1, cx1, cy1, cp1,
    rho0, dg0, u0, rho1, dg1, u1, tmp0, tmp1,
):
    nx, ny, nz = rhs.shape
    s, t = lax.axis_index("stream"), lax.axis_index("trans")
    groups = lax.axis_size("trans")
    s_even, t_even = s % 2 == 0, t % 2 == 0
    own = R0 + HALO
    full = nx + 2 * HALO
    zero0 = jnp.zeros((ROWS0, nz), F32)
    for i in range(full):
        rho0[i] = zero0
        b0[i] = zero0
    for i in range(nx):
        b0[HALO + i, pl.ds(own, ny), :] = rhs[i]
        rho0[HALO + i, pl.ds(own, ny), :] = dens[i]

    def sides(a, b):
        low = jnp.where(t_even, b, a)
        high = jnp.where(t_even, a, b)
        return jnp.where(t > 0, low, 0.0), jnp.where(t < groups - 1, high, 0.0)

    def near(ref, i, a, b):
        low, high = sides(a, b)
        ref[i, pl.ds(own - NEAR, NEAR), :] = low
        ref[i, pl.ds(own + ny, NEAR), :] = high

    def far(i, a, b):
        low, high = sides(a, b)
        b0[i, pl.ds(own - NEAR - FAR, FAR), :] = low[:FAR]
        b0[i, pl.ds(own + ny + NEAR, FAR), :] = high[:FAR]
        rho0[i, pl.ds(own - NEAR - FAR, FAR), :] = low[FAR:]
        rho0[i, pl.ds(own + ny + NEAR, FAR), :] = high[FAR:]

    for i in range(nx):
        near(b0, HALO + i, ya[i], yb[i])
        near(rho0, HALO + i, ya[nx + i], yb[nx + i])
        far(HALO + i, ya[2 * nx + i], yb[2 * nx + i])
    base = 0
    for x, high in ((xa, s_even), (xb, jnp.logical_not(s_even))):
        at_b = jnp.where(high, HALO + nx, HALO - HB)
        at_d = jnp.where(high, HALO + nx, HALO - HD)
        at_f = jnp.where(high, HALO + nx, HALO - FAR)
        for i in range(HB):
            b0[at_b + i, pl.ds(own, ny), :] = x[i]
            near(b0, at_b + i, ca[base + i], cb[base + i])
        for i in range(HD):
            rho0[at_d + i, pl.ds(own, ny), :] = x[HB + i]
            near(rho0, at_d + i, ca[base + HB + i], cb[base + HB + i])
        for i in range(FAR):
            k = base + HB + HD + i
            far(at_f + i, ca[k], cb[k])
        base += HB + HD + FAR
    wide = ny + 2 * HALO
    for i in range(nx + 2 * HB):
        at = HALO - HB + i
        b0[at, pl.ds(R0, wide), :] = b0[at, pl.ds(R0, wide), :] + source[i]

    f0 = (cx0, cy0, cp0)
    lo, hi = HALO - HB, HALO + nx + HB
    zero_row = jnp.zeros((1, nz), F32)
    for i in range(lo - 1, hi + 1):
        for ref in (u0, v0, cy0):
            ref[i, pl.ds(R0 - 1, 1), :] = zero_row
        for ref in (u0, v0):
            ref[i, pl.ds(R0 + wide, 1), :] = zero_row
    setup(rho0, f0, w0, dg0, lo, hi, R0, wide, 1, 0)
    start(u0, b0, w0, lo, hi, R0, wide)
    sweep(u0, v0, b0, w0, f0, lo + 1, hi - 1, R0, wide, 1)

    half = nx // 2 + HALO
    wide1 = 24
    zero1 = jnp.zeros((ROWS1, nz), F32)
    for i in range(half):
        for ref in (rho1, b1, u1, v1, cy1):
            ref[i] = zero1
    for i in range(half):
        tmp0[i] = zero0

    def rho_rows(i):
        return rho0[i, pl.ds(R0, wide), :]

    rows_to = SHIFT1
    coarsen(rho_rows, rho1, tmp0, (2, 1, half - 2), wide, 1, rows_to)

    def res_rows(i):
        return residual(v0, b0, dg0, f0, i, R0, wide, 1)

    coarsen(res_rows, b1, tmp0, (lo + 2, (lo + 2) // 2, (hi - lo - 4) // 2), wide, 1, rows_to)
    f1 = (cx1, cy1, cp1)
    lo1, hi1 = (lo + 2) // 2, (hi - 2) // 2
    setup(rho1, f1, w1, dg1, lo1, hi1, R1, wide1, 2, 1)
    start(u1, b1, w1, lo1, hi1, R1, wide1)
    sweep(u1, v1, b1, w1, f1, lo1 + 1, hi1 - 1, R1, wide1, 2)

    own1 = SHIFT1 + HALO // 2
    ny1 = ny // 2
    first1 = HALO // 2

    def packed(fine):
        total = None
        for k in range(nx // 4):
            a = first1 + 2 * k
            pairs = fine(a) + fine(a + 1)
            even = (lanes(pairs.shape) // 2) % 2 == 0
            pairs = pairs + jnp.where(even, up(pairs, 2), down(pairs, 2))
            turn = lanes(pairs.shape) % 4 == k
            total = jnp.where(turn, pairs, 0.0 if total is None else total)
        tmp1[...] = total
        return 0.125 * (tmp1[pl.ds(0, ny1 // 2, stride=2), :] + tmp1[pl.ds(1, ny1 // 2, stride=2), :])

    rows2 = ny1 // 2
    slots[0, pl.ds(0, rows2), :] = packed(
        lambda i: residual(v1, b1, dg1, f1, i, own1, ny1, 2)
    )
    slots[0, pl.ds(rows2, rows2), :] = packed(lambda i: rho1[i, pl.ds(own1, ny1), :])
    slot = slots[0]

    def put(g):
        slots[g] = slot

    over(1, slots.shape[0], put)


class Coarse:
    def __init__(self, k, refs, planes, rows, mult, nz):
        self.rho, self.cx, self.cy, self.cp, self.w, self.dg, self.b, self.va, self.vb = refs
        self.planes, self.rows = planes, rows
        self.pitch, self.mult, self.st = 1 << k, mult >> k, mult << k
        self.level = 2 + k
        lane = lanes((rows, nz))
        self.sub = (lane // self.pitch) % self.mult
        self.even_z = (lane // self.st) % 2 == 0
        self.first, self.last = lane < self.st, lane >= nz - self.st
        self.at = pl.ds(8, rows)

    def each(self, fn):
        over(1, 1 + self.planes, fn, 8, 2)

    def next_x(self, here, above):
        if self.mult == 1:
            return above
        far = down(above, (self.mult - 1) * self.pitch)
        return jnp.where(self.sub == self.mult - 1, far, up(here, self.pitch))

    def prev_x(self, here, below):
        if self.mult == 1:
            return below
        far = up(below, (self.mult - 1) * self.pitch)
        return jnp.where(self.sub == 0, far, down(here, self.pitch))

    def setup(self):
        scale = 2.0 * 0.25**self.level
        rho, cx, cy, cp, at, n = self.rho, self.cx, self.cy, self.cp, self.at, self.rows
        cx[0, at, :] = quotient(scale, self.next_x(rho[0, at, :], rho[1, at, :]))

        def plane(i):
            here = rho[i, at, :]
            fx = quotient(scale, here + self.next_x(here, rho[i + 1, at, :]))
            cx[i, at, :] = fx
            cy[i, pl.ds(0, n + 8), :] = quotient(
                scale, rho[i, pl.ds(0, n + 8), :] + rho[i, pl.ds(1, n + 8), :]
            )
            fp = quotient(scale, here + jnp.where(self.last, 0.0, up(here, self.st)))
            fm = jnp.where(self.first, quotient(scale, here), down(fp, self.st))
            cp[i, at, :] = jnp.where(self.last, 0.0, fp)
            diag = fx + self.prev_x(fx, cx[i - 1, at, :]) + fp + fm
            diag = diag + cy[i, at, :] + cy[i, pl.ds(7, n), :]
            self.dg[i, at, :] = diag
            self.w[i, at, :] = omega_factor / diag

        self.each(plane)

    def beside(self, v, i):
        at, n = self.at, self.rows
        here = v[i, at, :]
        fx, fz = self.cx[i, at, :], self.cp[i, at, :]
        total = fx * self.next_x(here, v[i + 1, at, :])
        total = total + self.prev_x(fx * here, self.cx[i - 1, at, :] * v[i - 1, at, :])
        total = total + self.cy[i, at, :] * v[i, pl.ds(9, n), :]
        total = total + self.cy[i, pl.ds(7, n), :] * v[i, pl.ds(7, n), :]
        return here, total + (fz * up(here, self.st) + down(fz * here, self.st))

    def start(self):
        def plane(i):
            self.va[i, self.at, :] = self.w[i, self.at, :] * self.b[i, self.at, :]

        self.each(plane)

    def smooth(self, n):
        for _ in range(n):

            def plane(i):
                here, total = self.beside(self.va, i)
                self.vb[i, self.at, :] = (1.0 - omega_factor) * here + self.w[i, self.at, :] * (
                    self.b[i, self.at, :] + total
                )

            self.each(plane)
            self.va, self.vb = self.vb, self.va

    def residual(self, i):
        here, total = self.beside(self.va, i)
        return self.b[i, self.at, :] + (total - self.dg[i, self.at, :] * here)

    def coarsen(self, fine, out, tmp):
        def plane(i):
            total = fine(i)
            even_x = self.sub % 2 == 0
            total = total + jnp.where(even_x, up(total, self.pitch), down(total, self.pitch))
            total = total + jnp.where(self.even_z, up(total, self.st), down(total, self.st))
            tmp[i, pl.ds(0, self.rows), :] = total
            half = self.rows // 2
            out[i, pl.ds(8, half), :] = 0.125 * (
                tmp[i, pl.ds(0, half, stride=2), :] + tmp[i, pl.ds(1, half, stride=2), :]
            )

        self.each(plane)

    def correct(self, below, tmp):
        def plane(i):
            doubled(tmp, i, 0, below.va[i, below.at, :])
            self.va[i, self.at, :] = self.va[i, self.at, :] + tmp[i, pl.ds(0, self.rows), :]

        self.each(plane)


def post_kernel(slots, v0, b0, w0, cx0, cy0, cp0, v1, b1, w1, cx1, cy1, cp1, out, *refs):
    nx, ny, nz = out.shape
    slabs, groups = lax.axis_size("stream"), lax.axis_size("trans")
    s, t = lax.axis_index("stream"), lax.axis_index("trans")
    gx, gy = nx // 4, ny // 4
    assert gx * (nz // 4) == nz
    rows = groups * gy
    levels = [Coarse(k, refs[9 * k : 9 * k + 9], slabs, rows >> k, gx, nz) for k in range(3)]
    tmp, e1, u1, x1, e0, u0, x0 = refs[27:]
    for c in levels:
        zero = jnp.zeros((c.rows + 16, nz), F32)

        def clear(i, group=(c.rho, c.va, c.vb), zero=zero):
            for ref in group:
                ref[i] = zero

        over(0, slabs + 2, clear)

    two, three, four = levels
    top = subs((8, nz)) < 4

    def unpack(sl):
        for pair in range(groups // 2):
            first = slots[sl * groups + 2 * pair]
            second = slots[sl * groups + 2 * pair + 1]
            to = pl.ds(8 + 8 * pair, 8)
            two.b[1 + sl, to, :] = jnp.where(top, first, pltpu.roll(second, 4, 0))
            two.rho[1 + sl, to, :] = jnp.where(top, pltpu.roll(first, 4, 0), second)

    over(0, slabs, unpack, 8, 2)
    two.setup()
    two.coarsen(lambda i: two.rho[i, two.at, :], three.rho, tmp)
    three.setup()
    three.coarsen(lambda i: three.rho[i, three.at, :], four.rho, tmp)
    four.setup()
    two.start()
    two.smooth(1)
    two.coarsen(two.residual, three.b, tmp)
    three.start()
    three.smooth(1)
    three.coarsen(three.residual, four.b, tmp)
    four.start()
    four.smooth(CSWEEPS - 1)
    three.correct(four, tmp)
    three.smooth(POST)
    two.correct(three, tmp)
    two.smooth(POST)

    f1 = (cx1, cy1, cp1)
    first1, nx1 = HALO // 2, nx // 2
    wide1 = 24
    for i in range(e1.shape[0]):
        e1[i] = jnp.zeros((ROWS1, nz), F32)
    zero_row = jnp.zeros((1, nz), F32)
    for i in range(u1.shape[0]):
        for ref in (u1, x1):
            ref[i, pl.ds(R1 - 1, 1), :] = zero_row
            ref[i, pl.ds(R1 + wide1, 1), :] = zero_row
    place = lanes((gy + 4, nz)) % gx
    around = [two.va[s + k, pl.ds(t * gy + 6, gy + 4), :] for k in range(3)]
    for k in range(gx + 4):
        plane, sub = around[(k + gx - 2) // gx], (k + gx - 2) % gx
        value = plane if sub == 0 else pltpu.roll(plane, nz - sub, 1)
        for m in range(1, gx):
            value = jnp.where(place == m, pltpu.roll(plane, (m - sub) % nz, 1) if m != sub else plane, value)
        doubled(e1, k, SHIFT1 + first1 - 4, value)
    rows1 = pl.ds(R1, wide1)
    for i in range(first1 - 3, first1 + nx1 + 3):
        u1[i, rows1, :] = v1[i, rows1, :] + e1[(i - first1 + 4) // 2, rows1, :]
    sweep(u1, x1, b1, w1, f1, first1 - 2, first1 + nx1 + 2, R1, wide1, 2)
    sweep(x1, u1, b1, w1, f1, first1 - 1, first1 + nx1 + 1, R1, wide1, 2)

    f0 = (cx0, cy0, cp0)
    own = R0 + HALO
    low, count = own - 8, ny + 16
    for k in range(nx1 + 2):
        value = u1[first1 - 1 + k, pl.ds(SHIFT1 + first1 - 4, ny // 2 + 8), :]
        doubled(e0, k, low, value)
    for i in range(HALO - 2, HALO + nx + 2):
        rows0 = pl.ds(low, count)
        u0[i, rows0, :] = v0[i, rows0, :] + e0[(i - HALO + 2) // 2, rows0, :]
    sweep(u0, x0, b0, w0, f0, HALO - 1, HALO + nx + 1, low + 7, count - 8, 1)
    for i in range(nx):
        out[i] = swept(x0, b0, w0, f0, HALO + i, own, ny, 1)


def exchange(count, parity, open_ends):
    pairs = []
    for i in range(count):
        j = ((i + parity) ^ 1) - parity
        if 0 <= j < count:
            pairs.append((i, j))
        elif not open_ends:
            pairs.append((i, count - 1 - i))
    return pairs


def swap(value, axis, parity, open_ends):
    count = lax.axis_size(axis)
    return lax.ppermute(value, axis, exchange(count, parity, open_ends))


def gather(value):
    return lax.all_to_all(value, AXES, 0, 0, tiled=True)


def sds(*shape):
    return jax.ShapeDtypeStruct(shape, F32)


def body(rhs, vof, disc_owner, disc_cell, disc_force):
    nx, ny, nz = rhs.shape
    slabs, groups = lax.axis_size("stream"), lax.axis_size("trans")
    devices = slabs * groups
    rows = disc_cell.shape[1] // nz
    wide = ny + 2 * HALO
    halo_x = sds(HB + HD, ny, nz)
    halo_y = sds(3 * nx, 8, nz)
    corner = sds(2 * (HB + HD + FAR), 8, nz)

    block, row = sds(nx, ny, nz), pltpu.VMEM((rows, nz), jnp.int32)
    rhs, dens, xa, xb, ya, yb, disc = pl.pallas_call(
        functools.partial(pack_kernel, devices),
        out_shape=(block, block, halo_x, halo_x, halo_y, halo_y, sds(devices * 2 * rows, nz)),
        in_specs=[pl.BlockSpec(memory_space=pltpu.MemorySpace.HBM)] * 5,
        scratch_shapes=[
            pltpu.VMEM((nx, ny, nz), jnp.int32),
            row,
            row,
            pltpu.VMEM((rows, nz), F32),
            pltpu.SemaphoreType.DMA((5,)),
        ],
        compiler_params=params(12),
        name="pack",
    )(
        *(
            pltpu.with_memory_space_constraint(x, pltpu.MemorySpace.HBM)
            for x in (
                rhs,
                vof,
                disc_owner.reshape(rows, nz),
                disc_cell.reshape(rows, nz),
                disc_force.reshape(rows, nz),
            )
        )
    )
    disc = gather(disc)
    xa = swap(xa, "stream", 0, True)
    xb = swap(xb, "stream", 1, True)
    ya = swap(ya, "trans", 0, False)
    yb = swap(yb, "trans", 1, False)
    ca, cb = pl.pallas_call(
        corner_kernel, out_shape=(corner, corner), compiler_params=params(8), name="corner"
    )(xa, xb)
    ca = swap(ca, "trans", 0, False)
    cb = swap(cb, "trans", 1, False)
    cols = groups * rows * nz
    source = pl.pallas_call(
        functools.partial(source_kernel, (nx, ny, nz)),
        out_shape=sds(nx + 2 * HB, wide, nz),
        scratch_shapes=[
            pltpu.VMEM((nx * wide, cols), BF16),
            pltpu.VMEM((3 * nz, cols), BF16),
        ],
        compiler_params=params(24),
        name="source",
    )(disc)
    full, half = nx + 2 * HALO, nx // 2 + HALO
    frame0, frame1 = sds(full, ROWS0, nz), sds(half, ROWS1, nz)
    s0, s1 = pltpu.VMEM(frame0.shape, F32), pltpu.VMEM(frame1.shape, F32)
    slots, *state = pl.pallas_call(
        pre_kernel,
        out_shape=(sds(devices, 8, nz), *([frame0] * 6), *([frame1] * 6)),
        scratch_shapes=[
            s0, s0, s0, s1, s1, s1,
            pltpu.VMEM((half, ROWS0, nz), F32), pltpu.VMEM((ny // 2, nz), F32),
        ],
        compiler_params=params(28),
        name="presmooth",
    )(rhs, dens, xa, xb, ya, yb, ca, cb, source)
    slots = gather(slots)
    gy = groups * ny // 4
    scratch = [pltpu.VMEM((slabs + 2, (gy >> k) + 16, nz), F32) for k in range(3) for _ in range(9)]
    scratch += [
        pltpu.VMEM((slabs + 2, gy, nz), F32),
        pltpu.VMEM((nx // 4 + 4, ROWS1, nz), F32),
        s1,
        s1,
        pltpu.VMEM((nx // 2 + 2, ROWS0, nz), F32),
        s0,
        s0,
    ]
    return pl.pallas_call(
        post_kernel,
        out_shape=sds(nx, ny, nz),
        scratch_shapes=scratch,
        compiler_params=params(28),
        name="postsmooth",
    )(slots, *state)


def solution(mesh):
    return jax.shard_map(
        body,
        mesh=mesh,
        in_specs=(
            P("stream", "trans", None),
            P("stream", "trans", None),
            P("stream", "trans", None),
            P("stream", "trans"),
            P("stream", "trans"),
        ),
        out_specs=P("stream", "trans", None),
        check_vma=False,
    )
```

```python
import functools

import jax
import jax.numpy as jnp
from jax import lax
from jax.experimental import pallas as pl
from jax.experimental.pallas import tpu as pltpu
from jax.sharding import PartitionSpec as P


POST = 2
CSWEEPS = 8

air_density = 0.0012
omega_factor = 0.8

F32 = jnp.float32
BF16 = jnp.bfloat16
AXES = ("stream", "trans")

HALO = 12
HB = 10
HD = 11
NEAR = 8
FAR = 4
R0 = 4
ROWS0 = 48
R1 = 12
ROWS1 = 40
SHIFT1 = 10


def params(mib):
    return pltpu.CompilerParams(vmem_limit_bytes=mib << 20)


def lanes(shape):
    return lax.broadcasted_iota(jnp.int32, shape, len(shape) - 1)


def subs(shape):
    return lax.broadcasted_iota(jnp.int32, shape, len(shape) - 2)


def log2(n):
    assert n & (n - 1) == 0
    return n.bit_length() - 1


def up(x, st):
    return pltpu.roll(x, x.shape[-1] - st, x.ndim - 1)


def down(x, st):
    return pltpu.roll(x, st, x.ndim - 1)


def over(lo, hi, fn, limit=64, step=4):
    def group(indices):
        stores = [store for i in indices for store in fn(i) or ()]
        for ref, index, value in stores:
            ref[index] = value

    if hi - lo <= limit:
        for i in range(lo, hi, step):
            group(range(i, min(i + step, hi)))
        return
    whole = (hi - lo) // step

    def chunk(k, carry):
        group([lo + k * step + j for j in range(step)])
        return carry

    lax.fori_loop(0, whole, chunk, 0)
    group(range(lo + whole * step, hi))


LEAST = 0.8 * air_density


MEAN = 0.125
DOWN = 4 * MEAN


def face(den):
    return 1.0 / jnp.maximum(den, LEAST)


def pair(a, b):
    a, b = jnp.maximum(a, LEAST), jnp.maximum(b, LEAST)
    both = 1.0 / (a * b)
    return both * b, both * a


def setup(rho, faces, w, dg, x0, x1, r0, nr, st):
    cx, cy, cp = faces
    nz = rho.shape[-1]
    rows = pl.ds(r0, nr)
    lane = lanes((nr, nz))
    first, last = lane < st, lane >= nz - st
    cx[x0 - 1, rows, :] = face(rho[x0 - 1, rows, :] + rho[x0, rows, :])

    def plane(i):
        here = rho[i, rows, :]
        fx, fy = pair(here + rho[i + 1, rows, :], here + rho[i, pl.ds(r0 + 1, nr), :])
        fp, alone = pair(here + jnp.where(last, 0.0, up(here, st)), here)
        fm = jnp.where(first, alone, down(fp, st))
        at = (i, rows)
        before = face(rho[i, pl.ds(r0 - 1, 1), :] + rho[i, pl.ds(r0, 1), :])
        return (
            (cy, (i, pl.ds(r0 - 1, 1)), before),
            (cx, at, fx),
            (cy, at, fy),
            (cp, at, jnp.where(last, 0.0, fp)),
            (dg, at, (fx + fy) + (fp + fm)),
        )

    over(x0, x1, plane, step=SETUP_STEP)

    def diagonal(i):
        at = (i, rows)
        diag = dg[at] + (cx[i - 1, rows, :] + cy[i, pl.ds(r0 - 1, nr), :])
        return (dg, at, diag), (w, at, jnp.where(rho[at] > 0.0, omega_factor / diag, 0.0))

    over(x0, x1, diagonal)


SETUP_STEP = 4


def beside(v, faces, i, r0, nr, st):
    cx, cy, cp = faces
    rows = pl.ds(r0, nr)
    here = v[i, rows, :]
    total = cx[i, rows, :] * v[i + 1, rows, :] + cx[i - 1, rows, :] * v[i - 1, rows, :]
    total = total + cy[i, rows, :] * v[i, pl.ds(r0 + 1, nr), :]
    total = total + cy[i, pl.ds(r0 - 1, nr), :] * v[i, pl.ds(r0 - 1, nr), :]
    fz = cp[i, rows, :]
    total = total + (fz * up(here, st) + down(fz * here, st))
    return here, total


def start(v, b, w, x0, x1, r0, nr):
    rows = pl.ds(r0, nr)

    def plane(i):
        return ((v, (i, rows), w[i, rows, :] * b[i, rows, :]),)

    over(x0, x1, plane)


def swept(v, b, w, faces, i, r0, nr, st):
    rows = pl.ds(r0, nr)
    here, total = beside(v, faces, i, r0, nr, st)
    return (1.0 - omega_factor) * here + w[i, rows, :] * (b[i, rows, :] + total)


def sweep(v, out, b, w, faces, x0, x1, r0, nr, st):
    def plane(i):
        return ((out, (i, pl.ds(r0, nr)), swept(v, b, w, faces, i, r0, nr, st)),)

    over(x0, x1, plane)


def residual(v, b, dg, faces, i, r0, nr, st):
    here, total = beside(v, faces, i, r0, nr, st)
    rows = pl.ds(r0, nr)
    return b[i, rows, :] + (total - dg[i, rows, :] * here)


def coarsen(factor, fine, out, tmp, pairs, nr, st, to):
    a0, c0, count = pairs
    half = nr // 2

    def planes(k):
        return ((tmp, (c0 + k, pl.ds(0, nr)), fine(a0 + 2 * k) + fine(a0 + 2 * k + 1)),)

    def means(k):
        c = c0 + k
        total = tmp[c, pl.ds(0, half, stride=2), :] + tmp[c, pl.ds(1, half, stride=2), :]
        even = (lanes(total.shape) // st) % 2 == 0
        total = total + jnp.where(even, up(total, st), down(total, st))
        return ((out, (c, pl.ds(to, half)), factor * total),)

    over(0, count, planes, step=2)
    over(0, count, means)


def doubled(ref, k, row, value):
    n = value.shape[0]
    ref[k, pl.ds(row, n, stride=2), :] = value
    ref[k, pl.ds(row + 1, n, stride=2), :] = value


def half_tile(a, b, upper):
    top = subs(a.shape) < FAR
    return jnp.where(
        upper,
        jnp.where(top, pltpu.roll(a, FAR, 0), b),
        jnp.where(top, a, pltpu.roll(b, FAR, 0)),
    )


def pack_kernel(groups, *refs):
    outside, (rhs, dens, xa, xb, ya, yb, disc) = refs[:5], refs[5:12]
    vof, owner, cell, force, sems = refs[12:]
    inside = (rhs, vof, owner, cell, force)
    copies = [
        pltpu.make_async_copy(a, b, sems.at[i]) for i, (a, b) in enumerate(zip(outside, inside))
    ]
    for copy in copies:
        copy.start()
    for copy in copies:
        copy.wait()
    nx, ny, nz = rhs.shape
    s_even = lax.axis_index("stream") % 2 == 0
    t_even = lax.axis_index("trans") % 2 == 0
    for i in range(nx):
        dens[i] = air_density + ((1.0 - air_density) / 1000.0) * vof[i].astype(F32)
    tail_b, tail_d = nx - HB, nx - HD
    for out, tail in ((xa, s_even), (xb, jnp.logical_not(s_even))):
        at_b, at_d = jnp.where(tail, tail_b, 0), jnp.where(tail, tail_d, 0)
        for i in range(HB):
            out[i] = rhs[at_b + i]
        for i in range(HD):
            out[HB + i] = dens[at_d + i]
    for i in range(nx):
        b, d = rhs[i], dens[i]
        mid_b, mid_d = b[FAR : FAR + 8], d[FAR : FAR + 8]
        for out, tail in ((ya, t_even), (yb, jnp.logical_not(t_even))):
            out[i] = jnp.where(tail, b[ny - NEAR :], b[:NEAR])
            out[nx + i] = jnp.where(tail, d[ny - NEAR :], d[:NEAR])
            out[2 * nx + i] = half_tile(mid_b, mid_d, jnp.logical_not(tail))
    key = (owner[...] * (nx * ny * nz) + cell[...]).astype(F32)
    rows = key.shape[0]
    values = jnp.concatenate([key, force[...]], axis=0)
    if 2 * rows < 8:
        values = jnp.concatenate([values] * (4 // rows), axis=0)
    for g in range(groups * 2 * rows // 8):
        disc[pl.ds(8 * g, 8), :] = values


def corner_kernel(xa, xb, ca, cb):
    ny = xa.shape[1]
    s_even = lax.axis_index("stream") % 2 == 0
    t_even = lax.axis_index("trans") % 2 == 0
    base = 0
    for x, high in ((xa, s_even), (xb, jnp.logical_not(s_even))):
        for i in range(HB + HD):
            tile = x[i]
            low_rows, high_rows = tile[:NEAR], tile[ny - NEAR :]
            ca[base + i] = jnp.where(t_even, high_rows, low_rows)
            cb[base + i] = jnp.where(t_even, low_rows, high_rows)
        at_b = jnp.where(high, 0, HB - FAR)
        at_d = jnp.where(high, HB, HB + HD - FAR)
        for i in range(FAR):
            mid_b = x[at_b + i, pl.ds(FAR, 8), :]
            mid_d = x[at_d + i, pl.ds(FAR, 8), :]
            ca[base + HB + HD + i] = half_tile(mid_b, mid_d, jnp.logical_not(t_even))
            cb[base + HB + HD + i] = half_tile(mid_b, mid_d, t_even)
        base += HB + HD + FAR


def source_kernel(shape, disc, out, hot, val):
    nx, ny, nz = shape
    slabs, groups = lax.axis_size("stream"), lax.axis_size("trans")
    s, t = lax.axis_index("stream"), lax.axis_index("trans")
    per_slab = disc.shape[0] // slabs
    part = per_slab // groups // 2
    frame = out.shape[1]
    cols = part * groups * nz
    side = (frame - ny) // 2
    for offset in (-1, 0, 1):
        planes = []
        for x in range(nx) if offset == 0 else range(nx - HB, nx) if offset < 0 else range(HB):
            gap = 0 if offset == 0 else nx - x if offset < 0 else x + 1
            edge = side if gap <= FAR else NEAR
            planes.append((x, x + HB + offset * nx, side - edge, ny + 2 * edge))
        slab = s + offset

        def fill(planes=planes, slab=slab):
            base = pl.multiple_of(slab * per_slab, 8)
            zrow = subs((nz, nz))
            yrow = subs((frame, nz))
            for g in range(groups):
                for p in range(part):
                    at = pl.ds((g * part + p) * nz, nz)
                    tile = disc[pl.ds(base + (g * 2 * part) // 8 * 8, 8), :]
                    r = (g * 2 * part) % 8 + p
                    key = tile[r : r + 1].astype(jnp.int32)
                    f = tile[r + part : r + part + 1]
                    z = key & (nz - 1)
                    y = (key >> log2(nz)) & (ny - 1)
                    x = (key >> log2(nz * ny)) & (nx - 1)
                    o = key >> log2(nz * ny * nx)
                    row = (o - t) * ny + y + side
                    in_row = jnp.where(yrow == row, 1.0, 0.0).astype(BF16)
                    in_near = None
                    if len({first for _, _, first, _ in planes}) > 1:
                        span = yrow[: ny + 2 * NEAR] + (side - NEAR)
                        in_near = jnp.where(span == row, 1.0, 0.0).astype(BF16)
                    to = 0
                    for plane, _, first, count in planes:
                        chosen = jnp.where(x == plane, 1.0, 0.0)
                        chosen = jnp.broadcast_to(chosen, (16, nz)).astype(BF16)
                        for k in range(count // 16):
                            of = in_row if first % 16 == 0 else in_near
                            row_at = first + 16 * k if first % 16 == 0 else 16 * k
                            piece = of[row_at : row_at + 16]
                            hot[pl.ds(to, 16), at] = piece * chosen
                            to += 16
                    hi = f.astype(BF16).astype(F32)
                    here = zrow == z
                    for q, part_of in enumerate((hi, f - hi)):
                        val[pl.ds(q * nz, nz), at] = jnp.where(here, part_of, 0.0).astype(BF16)
            total = sum(count for _, _, _, count in planes)
            got = lax.dot_general(
                hot[pl.ds(0, total), pl.ds(0, cols)],
                val[:, pl.ds(0, cols)],
                (((1,), (1,)), ((), ())),
                preferred_element_type=F32,
            )
            got = got[:, :nz] + got[:, nz:]
            at = 0
            for _, to, first, count in planes:
                out[to, pl.ds(first, count), :] = got[at : at + count]
                at += count

        if offset == 0:
            fill()
        else:
            inside = slab >= 0 if offset < 0 else slab < slabs
            pl.when(inside)(fill)

            @pl.when(jnp.logical_not(inside))
            def _(planes=planes):
                for _, to, first, count in planes:
                    out[to, pl.ds(first, count), :] = jnp.zeros((count, nz), F32)


def pre_kernel(
    rhs, dens, xa, xb, ya, yb, ca, cb, source,
    slots, v0, b0, w0, cx0, cy0, cp0, v1, b1, w1, cx1, cy1, cp1,
    rho0, dg0, u0, rho1, dg1, u1, tmp0, tmp1,
):
    nx, ny, nz = rhs.shape
    s, t = lax.axis_index("stream"), lax.axis_index("trans")
    groups = lax.axis_size("trans")
    s_even, t_even = s % 2 == 0, t % 2 == 0
    own = R0 + HALO
    full = nx + 2 * HALO
    zero0 = jnp.zeros((ROWS0, nz), F32)
    for i in range(full):
        rho0[i] = zero0
        b0[i] = zero0
    for i in range(nx):
        b0[HALO + i, pl.ds(own, ny), :] = rhs[i]
        rho0[HALO + i, pl.ds(own, ny), :] = dens[i]

    def sides(a, b):
        low = jnp.where(t_even, b, a)
        high = jnp.where(t_even, a, b)
        return jnp.where(t > 0, low, 0.0), jnp.where(t < groups - 1, high, 0.0)

    def near(ref, i, a, b):
        low, high = sides(a, b)
        ref[i, pl.ds(own - NEAR, NEAR), :] = low
        ref[i, pl.ds(own + ny, NEAR), :] = high

    def far(i, a, b):
        low, high = sides(a, b)
        b0[i, pl.ds(own - NEAR - FAR, FAR), :] = low[:FAR]
        b0[i, pl.ds(own + ny + NEAR, FAR), :] = high[:FAR]
        rho0[i, pl.ds(own - NEAR - FAR, FAR), :] = low[FAR:]
        rho0[i, pl.ds(own + ny + NEAR, FAR), :] = high[FAR:]

    for i in range(nx):
        near(b0, HALO + i, ya[i], yb[i])
        near(rho0, HALO + i, ya[nx + i], yb[nx + i])
        far(HALO + i, ya[2 * nx + i], yb[2 * nx + i])
    base = 0
    for x, high in ((xa, s_even), (xb, jnp.logical_not(s_even))):
        at_b = jnp.where(high, HALO + nx, HALO - HB)
        at_d = jnp.where(high, HALO + nx, HALO - HD)
        at_f = jnp.where(high, HALO + nx, HALO - FAR)
        for i in range(HB):
            b0[at_b + i, pl.ds(own, ny), :] = x[i]
            near(b0, at_b + i, ca[base + i], cb[base + i])
        for i in range(HD):
            rho0[at_d + i, pl.ds(own, ny), :] = x[HB + i]
            near(rho0, at_d + i, ca[base + HB + i], cb[base + HB + i])
        for i in range(FAR):
            k = base + HB + HD + i
            far(at_f + i, ca[k], cb[k])
        base += HB + HD + FAR
    wide = ny + 2 * HALO
    for i in range(nx + 2 * HB):
        at = HALO - HB + i
        gap = max(HALO - at, at - HALO - nx + 1)
        rows = pl.ds(0, ROWS0) if gap <= FAR else pl.ds(own - NEAR, ny + 2 * NEAR)
        b0[at, rows, :] = 0.5 * (b0[at, rows, :] + source[i, rows, :])

    f0 = (cx0, cy0, cp0)
    lo, hi = HALO - HB, HALO + nx + HB
    zero_row = jnp.zeros((1, nz), F32)
    for i in range(lo - 1, hi + 1):
        for ref in (u0, v0, cy0):
            ref[i, pl.ds(R0 - 1, 1), :] = zero_row
        for ref in (u0, v0):
            ref[i, pl.ds(R0 + wide, 1), :] = zero_row
    setup(rho0, f0, w0, dg0, lo, hi, R0, wide, 1)
    start(u0, b0, w0, lo, hi, R0, wide)
    inner, outer = HALO - 2, HALO + nx + 2
    for x0, x1, cut in ((lo + 1, inner, 4), (inner, outer, 0), (outer, hi - 1, 4)):
        sweep(u0, v0, b0, w0, f0, x0, x1, R0 + cut, wide - 2 * cut, 1)

    half = nx // 2 + HALO
    wide1 = 16
    zero1 = jnp.zeros((ROWS1, nz), F32)
    for i in range(half):
        for ref in (rho1, b1, u1, v1, cy1):
            ref[i] = zero1
    for i in range(half):
        tmp0[i] = zero0

    def rho_rows(i):
        return rho0[i, pl.ds(R0, wide), :]

    rows_to = SHIFT1
    coarsen(MEAN, rho_rows, rho1, tmp0, (2, 1, half - 2), wide, 1, rows_to)

    for x0, x1, cut in ((lo + 2, HALO - 4, 8), (HALO - 4, HALO + nx + 4, 4), (HALO + nx + 4, hi - 2, 8)):

        def res_rows(i, cut=cut):
            return residual(v0, b0, dg0, f0, i, R0 + cut, wide - 2 * cut, 1)

        pairs = (x0, x0 // 2, (x1 - x0) // 2)
        coarsen(DOWN, res_rows, b1, tmp0, pairs, wide - 2 * cut, 1, rows_to + cut // 2)
    f1 = (cx1, cy1, cp1)
    lo1, hi1 = (lo + 2) // 2, (hi - 2) // 2
    setup(rho1, f1, w1, dg1, lo1, hi1, R1, wide1, 2)
    start(u1, b1, w1, lo1, hi1, R1, wide1)
    sweep(u1, v1, b1, w1, f1, lo1 + 1, hi1 - 1, R1, wide1, 2)

    own1 = SHIFT1 + HALO // 2
    ny1 = ny // 2
    first1 = HALO // 2

    def packed(factor, fine):
        value = None
        for k in range(nx // 4):
            tmp1[k] = fine(first1 + 2 * k) + fine(first1 + 2 * k + 1)
        for k in range(nx // 4):
            total = tmp1[k, pl.ds(0, ny1 // 2, stride=2), :] + tmp1[k, pl.ds(1, ny1 // 2, stride=2), :]
            even = (lanes(total.shape) // 2) % 2 == 0
            total = total + jnp.where(even, up(total, 2), down(total, 2))
            turn = lanes(total.shape) % 4 == k
            value = jnp.where(turn, total, 0.0 if value is None else value)
        return factor * value

    rows2 = ny1 // 2
    slots[0, pl.ds(0, rows2), :] = packed(
        DOWN, lambda i: residual(v1, b1, dg1, f1, i, own1, ny1, 2)
    )
    slots[0, pl.ds(rows2, rows2), :] = packed(MEAN, lambda i: rho1[i, pl.ds(own1, ny1), :])
    slot = slots[0]

    def put(g):
        slots[g] = slot

    over(1, slots.shape[0], put)


class Coarse:
    def __init__(self, k, refs, planes, rows, mult, nz):
        self.rho, self.cx, self.cy, self.cp, self.w, self.dg, self.b, self.va, self.vb = refs
        self.planes, self.rows = planes, rows
        self.pitch, self.mult, self.st = 1 << k, mult >> k, mult << k
        lane = lanes((rows, nz))
        self.sub = (lane // self.pitch) % self.mult
        self.even_z = (lane // self.st) % 2 == 0
        self.first, self.last = lane < self.st, lane >= nz - self.st
        self.at = pl.ds(8, rows)

    def each(self, fn):
        over(1, 1 + self.planes, fn, 8, 4)

    def next_x(self, here, above):
        if self.mult == 1:
            return above
        far = down(above, (self.mult - 1) * self.pitch)
        return jnp.where(self.sub == self.mult - 1, far, up(here, self.pitch))

    def prev_x(self, here, below):
        if self.mult == 1:
            return below
        far = up(below, (self.mult - 1) * self.pitch)
        return jnp.where(self.sub == 0, far, down(here, self.pitch))

    def setup(self):
        rho, cx, cy, cp, at, n = self.rho, self.cx, self.cy, self.cp, self.at, self.rows
        cx[0, at, :] = face(self.next_x(rho[0, at, :], rho[1, at, :]))

        def plane(i):
            here = rho[i, at, :]
            fx, fy = pair(
                here + self.next_x(here, rho[i + 1, at, :]), here + rho[i, pl.ds(9, n), :]
            )
            fp, alone = pair(here + jnp.where(self.last, 0.0, up(here, self.st)), here)
            fm = jnp.where(self.first, alone, down(fp, self.st))
            return (
                (cx, (i, at), fx),
                (cy, (i, at), fy),
                (cy, (i, pl.ds(7, 1)), face(rho[i, pl.ds(8, 1), :])),
                (cp, (i, at), jnp.where(self.last, 0.0, fp)),
                (self.dg, (i, at), (fx + fy) + (fp + fm)),
            )

        self.each(plane)

        def diagonal(i):
            diag = self.prev_x(cx[i, at, :], cx[i - 1, at, :]) + cy[i, pl.ds(7, n), :]
            diag = self.dg[i, at, :] + diag
            return (self.dg, (i, at), diag), (self.w, (i, at), omega_factor / diag)

        self.each(diagonal)

    def beside(self, v, i):
        at, n = self.at, self.rows
        here = v[i, at, :]
        fx, fz = self.cx[i, at, :], self.cp[i, at, :]
        total = fx * self.next_x(here, v[i + 1, at, :])
        total = total + self.prev_x(fx * here, self.cx[i - 1, at, :] * v[i - 1, at, :])
        total = total + self.cy[i, at, :] * v[i, pl.ds(9, n), :]
        total = total + self.cy[i, pl.ds(7, n), :] * v[i, pl.ds(7, n), :]
        return here, total + (fz * up(here, self.st) + down(fz * here, self.st))

    def start(self):
        def plane(i):
            return ((self.va, (i, self.at), self.w[i, self.at, :] * self.b[i, self.at, :]),)

        self.each(plane)

    def smooth(self, n):
        for _ in range(n):

            def plane(i):
                here, total = self.beside(self.va, i)
                new = self.w[i, self.at, :] * (self.b[i, self.at, :] + total)
                return ((self.vb, (i, self.at), (1.0 - omega_factor) * here + new),)

            self.each(plane)
            self.va, self.vb = self.vb, self.va

    def residual(self, i):
        here, total = self.beside(self.va, i)
        return self.b[i, self.at, :] + (total - self.dg[i, self.at, :] * here)

    def coarsen(self, factor, fine, out, tmp):
        half = self.rows // 2

        def means(i):
            total = tmp[i, pl.ds(0, half, stride=2), :] + tmp[i, pl.ds(1, half, stride=2), :]
            even_x, even_z = self.sub[:half] % 2 == 0, self.even_z[:half]
            total = total + jnp.where(even_x, up(total, self.pitch), down(total, self.pitch))
            total = total + jnp.where(even_z, up(total, self.st), down(total, self.st))
            return ((out, (i, pl.ds(8, half)), factor * total),)

        self.each(lambda i: ((tmp, (i, pl.ds(0, self.rows)), fine(i)),))
        self.each(means)

    def correct(self, below, tmp):
        self.each(lambda i: doubled(tmp, i, 0, below.va[i, below.at, :]))
        self.each(
            lambda i: (
                (
                    self.va,
                    (i, self.at),
                    self.va[i, self.at, :] + tmp[i, pl.ds(0, self.rows), :],
                ),
            )
        )


def post_kernel(slots, v0, b0, w0, cx0, cy0, cp0, v1, b1, w1, cx1, cy1, cp1, out, *refs):
    nx, ny, nz = out.shape
    slabs, groups = lax.axis_size("stream"), lax.axis_size("trans")
    s, t = lax.axis_index("stream"), lax.axis_index("trans")
    gx, gy = nx // 4, ny // 4
    assert gx * (nz // 4) == nz
    rows = groups * gy
    levels = [Coarse(k, refs[9 * k : 9 * k + 9], slabs, rows >> k, gx, nz) for k in range(3)]
    tmp, e1, u1, x1, e0, u0, x0 = refs[27:]
    for c in levels:
        zero = jnp.zeros((c.rows + 16, nz), F32)

        def clear(i, group=(c.rho, c.va, c.vb), zero=zero):
            for ref in group:
                ref[i] = zero

        over(0, slabs + 2, clear)

    two, three, four = levels
    top = subs((8, nz)) < 4

    def unpack(sl):
        for pair in range(groups // 2):
            first = slots[sl * groups + 2 * pair]
            second = slots[sl * groups + 2 * pair + 1]
            to = pl.ds(8 + 8 * pair, 8)
            two.b[1 + sl, to, :] = jnp.where(top, first, pltpu.roll(second, 4, 0))
            two.rho[1 + sl, to, :] = jnp.where(top, pltpu.roll(first, 4, 0), second)

    over(0, slabs, unpack, 8, 2)
    two.setup()
    two.coarsen(MEAN, lambda i: two.rho[i, two.at, :], three.rho, tmp)
    three.setup()
    three.coarsen(MEAN, lambda i: three.rho[i, three.at, :], four.rho, tmp)
    four.setup()
    two.start()
    two.smooth(1)
    two.coarsen(DOWN, two.residual, three.b, tmp)
    three.start()
    three.smooth(1)
    three.coarsen(DOWN, three.residual, four.b, tmp)
    four.start()
    four.smooth(CSWEEPS - 1)
    three.correct(four, tmp)
    three.smooth(POST)
    two.correct(three, tmp)
    two.smooth(POST)

    f1 = (cx1, cy1, cp1)
    first1, nx1 = HALO // 2, nx // 2
    wide1 = 16
    for i in range(e1.shape[0]):
        e1[i] = jnp.zeros((ROWS1, nz), F32)
    zero_row = jnp.zeros((1, nz), F32)
    for i in range(u1.shape[0]):
        for ref in (u1, x1):
            ref[i, pl.ds(R1 - 1, 1), :] = zero_row
            ref[i, pl.ds(R1 + wide1, 1), :] = zero_row
    place = lanes((gy + 4, nz)) % gx
    around = [two.va[s + k, pl.ds(t * gy + 6, gy + 4), :] for k in range(3)]
    for k in range(gx + 4):
        plane, sub = around[(k + gx - 2) // gx], (k + gx - 2) % gx
        value = plane if sub == 0 else pltpu.roll(plane, nz - sub, 1)
        for m in range(1, gx):
            value = jnp.where(place == m, pltpu.roll(plane, (m - sub) % nz, 1) if m != sub else plane, value)
        doubled(e1, k, SHIFT1 + first1 - 4, value)
    rows1 = pl.ds(R1, wide1)
    for i in range(first1 - 3, first1 + nx1 + 3):
        u1[i, rows1, :] = v1[i, rows1, :] + e1[(i - first1 + 4) // 2, rows1, :]
    sweep(u1, x1, b1, w1, f1, first1 - 2, first1 + nx1 + 2, R1, wide1, 2)
    sweep(x1, u1, b1, w1, f1, first1 - 1, first1 + nx1 + 1, R1, wide1, 2)

    f0 = (cx0, cy0, cp0)
    own = R0 + HALO
    low, count = own - 4, ny + 8
    for k in range(nx1 + 2):
        value = u1[first1 - 1 + k, pl.ds(SHIFT1 + first1 - 4, ny // 2 + 8), :]
        doubled(e0, k, own - 8, value)
    for i in range(HALO - 2, HALO + nx + 2):
        rows0 = pl.ds(low, count)
        u0[i, rows0, :] = v0[i, rows0, :] + e0[(i - HALO + 2) // 2, rows0, :]
    sweep(u0, x0, b0, w0, f0, HALO - 1, HALO + nx + 1, low, count, 1)
    for i in range(nx):
        out[i] = swept(x0, b0, w0, f0, HALO + i, own, ny, 1)


def exchange(count, parity, open_ends):
    pairs = []
    for i in range(count):
        j = ((i + parity) ^ 1) - parity
        if 0 <= j < count:
            pairs.append((i, j))
        elif not open_ends:
            pairs.append((i, count - 1 - i))
    return pairs


def swap(value, axis, parity, open_ends):
    count = lax.axis_size(axis)
    return lax.ppermute(value, axis, exchange(count, parity, open_ends))


def gather(value):
    return lax.all_to_all(value, AXES, 0, 0, tiled=True)


def sds(*shape):
    return jax.ShapeDtypeStruct(shape, F32)


def body(rhs, vof, disc_owner, disc_cell, disc_force):
    nx, ny, nz = rhs.shape
    slabs, groups = lax.axis_size("stream"), lax.axis_size("trans")
    devices = slabs * groups
    rows = disc_cell.shape[1] // nz
    halo_x = sds(HB + HD, ny, nz)
    halo_y = sds(3 * nx, 8, nz)
    corner = sds(2 * (HB + HD + FAR), 8, nz)

    block, row = sds(nx, ny, nz), pltpu.VMEM((rows, nz), jnp.int32)
    rhs, dens, xa, xb, ya, yb, disc = pl.pallas_call(
        functools.partial(pack_kernel, devices),
        out_shape=(block, block, halo_x, halo_x, halo_y, halo_y, sds(devices * 2 * rows, nz)),
        in_specs=[pl.BlockSpec(memory_space=pltpu.MemorySpace.HBM)] * 5,
        scratch_shapes=[
            pltpu.VMEM((nx, ny, nz), jnp.int32),
            row,
            row,
            pltpu.VMEM((rows, nz), F32),
            pltpu.SemaphoreType.DMA((5,)),
        ],
        compiler_params=params(12),
        name="pack",
    )(
        *(
            pltpu.with_memory_space_constraint(x, pltpu.MemorySpace.HBM)
            for x in (
                rhs,
                vof,
                disc_owner.reshape(rows, nz),
                disc_cell.reshape(rows, nz),
                disc_force.reshape(rows, nz),
            )
        )
    )
    disc = gather(disc)
    xa = swap(xa, "stream", 0, True)
    xb = swap(xb, "stream", 1, True)
    ya = swap(ya, "trans", 0, False)
    yb = swap(yb, "trans", 1, False)
    ca, cb = pl.pallas_call(
        corner_kernel, out_shape=(corner, corner), compiler_params=params(8), name="corner"
    )(xa, xb)
    ca = swap(ca, "trans", 0, False)
    cb = swap(cb, "trans", 1, False)
    cols = groups * rows * nz
    source = pl.pallas_call(
        functools.partial(source_kernel, (nx, ny, nz)),
        out_shape=sds(nx + 2 * HB, ROWS0, nz),
        scratch_shapes=[
            pltpu.VMEM((nx * ROWS0, cols), BF16),
            pltpu.VMEM((2 * nz, cols), BF16),
        ],
        compiler_params=params(24),
        name="source",
    )(disc)
    full, half = nx + 2 * HALO, nx // 2 + HALO
    frame0, frame1 = sds(full, ROWS0, nz), sds(half, ROWS1, nz)
    s0, s1 = pltpu.VMEM(frame0.shape, F32), pltpu.VMEM(frame1.shape, F32)
    slots, *state = pl.pallas_call(
        pre_kernel,
        out_shape=(sds(devices, 8, nz), *([frame0] * 6), *([frame1] * 6)),
        scratch_shapes=[
            s0, s0, s0, s1, s1, s1,
            pltpu.VMEM((half, ROWS0, nz), F32), pltpu.VMEM((nx // 4, ny // 2, nz), F32),
        ],
        compiler_params=params(28),
        name="presmooth",
    )(rhs, dens, xa, xb, ya, yb, ca, cb, source)
    slots = gather(slots)
    gy = groups * ny // 4
    scratch = [pltpu.VMEM((slabs + 2, (gy >> k) + 16, nz), F32) for k in range(3) for _ in range(9)]
    scratch += [
        pltpu.VMEM((slabs + 2, gy, nz), F32),
        pltpu.VMEM((nx // 4 + 4, ROWS1, nz), F32),
        s1,
        s1,
        pltpu.VMEM((nx // 2 + 2, ROWS0, nz), F32),
        s0,
        s0,
    ]
    return pl.pallas_call(
        post_kernel,
        out_shape=sds(nx, ny, nz),
        scratch_shapes=scratch,
        compiler_params=params(32),
        name="postsmooth",
    )(slots, *state)


def solution(mesh):
    return jax.shard_map(
        body,
        mesh=mesh,
        in_specs=(
            P("stream", "trans", None),
            P("stream", "trans", None),
            P("stream", "trans", None),
            P("stream", "trans"),
            P("stream", "trans"),
        ),
        out_specs=P("stream", "trans", None),
        check_vma=False,
    )
```

```python
import functools

import jax
import jax.numpy as jnp
from jax import lax
from jax.experimental import pallas as pl
from jax.experimental.pallas import tpu as pltpu
from jax.sharding import PartitionSpec as P


POST = 2
CSWEEPS = 8

air_density = 0.0012
omega_factor = 0.8

F32 = jnp.float32
BF16 = jnp.bfloat16
AXES = ("stream", "trans")

HALO = 12
HB = 10
HD = 11
NEAR = 8
FAR = 4
THIN = 3
CORNER = HB + HD - THIN + FAR
R0 = 4
ROWS0 = 48
R1 = 12
ROWS1 = 40
SHIFT1 = 10


def params(mib):
    return pltpu.CompilerParams(vmem_limit_bytes=mib << 20)


def lanes(shape):
    return lax.broadcasted_iota(jnp.int32, shape, len(shape) - 1)


def subs(shape):
    return lax.broadcasted_iota(jnp.int32, shape, len(shape) - 2)


def log2(n):
    assert n & (n - 1) == 0
    return n.bit_length() - 1


def up(x, st):
    return pltpu.roll(x, x.shape[-1] - st, x.ndim - 1)


def down(x, st):
    return pltpu.roll(x, st, x.ndim - 1)


def over(lo, hi, fn, limit=64, step=4):
    def group(indices):
        stores = [store for i in indices for store in fn(i) or ()]
        for ref, index, value in stores:
            ref[index] = value

    if hi - lo <= limit:
        for i in range(lo, hi, step):
            group(range(i, min(i + step, hi)))
        return
    whole = (hi - lo) // step

    def chunk(k, carry):
        group([lo + k * step + j for j in range(step)])
        return carry

    lax.fori_loop(0, whole, chunk, 0)
    group(range(lo + whole * step, hi))


LEAST = 0.8 * air_density


MEAN = 0.125
DOWN = 4 * MEAN


def face(den):
    return 1.0 / jnp.maximum(den, LEAST)


def pair(a, b):
    a, b = jnp.maximum(a, LEAST), jnp.maximum(b, LEAST)
    both = 1.0 / (a * b)
    return both * b, both * a


def setup(rho, faces, w, dg, x0, x1, r0, nr, st):
    cx, cy, cp = faces
    nz = rho.shape[-1]
    rows = pl.ds(r0, nr)
    lane = lanes((nr, nz))
    first, last = lane < st, lane >= nz - st
    cx[x0 - 1, rows, :] = face(rho[x0 - 1, rows, :] + rho[x0, rows, :])

    def plane(i):
        here = rho[i, rows, :]
        fx, fy = pair(here + rho[i + 1, rows, :], here + rho[i, pl.ds(r0 + 1, nr), :])
        fp, alone = pair(here + jnp.where(last, 0.0, up(here, st)), here)
        fm = jnp.where(first, alone, down(fp, st))
        at = (i, rows)
        before = face(rho[i, pl.ds(r0 - 1, 1), :] + rho[i, pl.ds(r0, 1), :])
        return (
            (cy, (i, pl.ds(r0 - 1, 1)), before),
            (cx, at, fx),
            (cy, at, fy),
            (cp, at, jnp.where(last, 0.0, fp)),
            (dg, at, (fx + fy) + (fp + fm)),
        )

    over(x0, x1, plane, step=SETUP_STEP)

    def diagonal(i):
        at = (i, rows)
        diag = dg[at] + (cx[i - 1, rows, :] + cy[i, pl.ds(r0 - 1, nr), :])
        return (dg, at, diag), (w, at, jnp.where(rho[at] > 0.0, omega_factor / diag, 0.0))

    over(x0, x1, diagonal)


SETUP_STEP = 4


def beside(v, faces, i, r0, nr, st):
    cx, cy, cp = faces
    rows = pl.ds(r0, nr)
    here = v[i, rows, :]
    total = cx[i, rows, :] * v[i + 1, rows, :] + cx[i - 1, rows, :] * v[i - 1, rows, :]
    total = total + cy[i, rows, :] * v[i, pl.ds(r0 + 1, nr), :]
    total = total + cy[i, pl.ds(r0 - 1, nr), :] * v[i, pl.ds(r0 - 1, nr), :]
    fz = cp[i, rows, :]
    total = total + (fz * up(here, st) + down(fz * here, st))
    return here, total


def start(v, b, w, x0, x1, r0, nr):
    rows = pl.ds(r0, nr)

    def plane(i):
        return ((v, (i, rows), w[i, rows, :] * b[i, rows, :]),)

    over(x0, x1, plane)


def swept(v, b, w, faces, i, r0, nr, st):
    rows = pl.ds(r0, nr)
    here, total = beside(v, faces, i, r0, nr, st)
    return (1.0 - omega_factor) * here + w[i, rows, :] * (b[i, rows, :] + total)


def sweep(v, out, b, w, faces, x0, x1, r0, nr, st):
    def plane(i):
        return ((out, (i, pl.ds(r0, nr)), swept(v, b, w, faces, i, r0, nr, st)),)

    over(x0, x1, plane)


def residual(v, b, dg, faces, i, r0, nr, st):
    here, total = beside(v, faces, i, r0, nr, st)
    rows = pl.ds(r0, nr)
    return b[i, rows, :] + (total - dg[i, rows, :] * here)


def coarsen(factor, fine, out, tmp, pairs, nr, st, to):
    a0, c0, count = pairs
    half = nr // 2

    def planes(k):
        return ((tmp, (c0 + k, pl.ds(0, nr)), fine(a0 + 2 * k) + fine(a0 + 2 * k + 1)),)

    def means(k):
        c = c0 + k
        total = tmp[c, pl.ds(0, half, stride=2), :] + tmp[c, pl.ds(1, half, stride=2), :]
        even = (lanes(total.shape) // st) % 2 == 0
        total = total + jnp.where(even, up(total, st), down(total, st))
        return ((out, (c, pl.ds(to, half)), factor * total),)

    over(0, count, planes, step=2)
    over(0, count, means)


def doubled(ref, k, row, value):
    n = value.shape[0]
    ref[k, pl.ds(row, n, stride=2), :] = value
    ref[k, pl.ds(row + 1, n, stride=2), :] = value


def half_tile(a, b, upper):
    top = subs(a.shape) < FAR
    return jnp.where(
        upper,
        jnp.where(top, pltpu.roll(a, FAR, 0), b),
        jnp.where(top, a, pltpu.roll(b, FAR, 0)),
    )


def pack_kernel(groups, *refs):
    outside, (rhs, dens, xa, xb, ya, yb, disc) = refs[:5], refs[5:12]
    vof, owner, cell, force, sems = refs[12:]
    inside = (rhs, vof, owner, cell, force)
    copies = [
        pltpu.make_async_copy(a, b, sems.at[i]) for i, (a, b) in enumerate(zip(outside, inside))
    ]
    for copy in copies:
        copy.start()
    for copy in copies:
        copy.wait()
    nx, ny, nz = rhs.shape
    s_even = lax.axis_index("stream") % 2 == 0
    t_even = lax.axis_index("trans") % 2 == 0
    for i in range(nx):
        dens[i] = air_density + ((1.0 - air_density) / 1000.0) * vof[i].astype(F32)
    tail_b, tail_d = nx - HB, nx - HD
    for out, tail in ((xa, s_even), (xb, jnp.logical_not(s_even))):
        at_b, at_d = jnp.where(tail, tail_b, 0), jnp.where(tail, tail_d, 0)
        for i in range(HB):
            out[i] = rhs[at_b + i]
        for i in range(HD):
            out[HB + i] = dens[at_d + i]
    for i in range(nx):
        b, d = rhs[i], dens[i]
        mid_b, mid_d = b[FAR : FAR + 8], d[FAR : FAR + 8]
        for out, tail in ((ya, t_even), (yb, jnp.logical_not(t_even))):
            out[i] = jnp.where(tail, b[ny - NEAR :], b[:NEAR])
            out[nx + i] = jnp.where(tail, d[ny - NEAR :], d[:NEAR])
            out[2 * nx + i] = half_tile(mid_b, mid_d, jnp.logical_not(tail))
    key = (owner[...] * (nx * ny * nz) + cell[...]).astype(F32)
    rows = key.shape[0]
    values = jnp.concatenate([key, force[...]], axis=0)
    if 2 * rows < 8:
        values = jnp.concatenate([values] * (4 // rows), axis=0)
    for g in range(groups * 2 * rows // 8):
        disc[pl.ds(8 * g, 8), :] = values


def corner_kernel(xa, xb, ca, cb):
    ny = xa.shape[1]
    s_even = lax.axis_index("stream") % 2 == 0
    t_even = lax.axis_index("trans") % 2 == 0
    base = 0
    for x, high in ((xa, s_even), (xb, jnp.logical_not(s_even))):

        def rows(i):
            tile = x[i]
            low_rows, high_rows = tile[:NEAR], tile[ny - NEAR :]
            return jnp.where(t_even, high_rows, low_rows), jnp.where(t_even, low_rows, high_rows)

        at = base
        for first, count in ((0, HB), (HB, HD)):
            of = first + jnp.where(high, 0, THIN)
            for i in range(count - THIN):
                ca[at], cb[at] = rows(of + i)
                at += 1
        for i in range(THIN):
            b = rows(jnp.where(high, HB - THIN + i, THIN - 1 - i))
            d = rows(HB + jnp.where(high, HD - THIN + i, THIN - 1 - i))
            ca[at] = half_tile(b[0], d[0], t_even)
            cb[at] = half_tile(b[1], d[1], jnp.logical_not(t_even))
            at += 1
        at_b = jnp.where(high, 0, HB - FAR)
        at_d = jnp.where(high, HB, HB + HD - FAR)
        for i in range(FAR):
            mid_b = x[at_b + i, pl.ds(FAR, 8), :]
            mid_d = x[at_d + i, pl.ds(FAR, 8), :]
            ca[at + i] = half_tile(mid_b, mid_d, jnp.logical_not(t_even))
            cb[at + i] = half_tile(mid_b, mid_d, t_even)
        base += CORNER


def source_kernel(shape, disc, out, hot, val):
    nx, ny, nz = shape
    slabs, groups = lax.axis_size("stream"), lax.axis_size("trans")
    s, t = lax.axis_index("stream"), lax.axis_index("trans")
    per_slab = disc.shape[0] // slabs
    part = per_slab // groups // 2
    frame = out.shape[1]
    cols = part * groups * nz
    side = (frame - ny) // 2
    for offset in (-1, 0, 1):
        planes = []
        for x in range(nx) if offset == 0 else range(nx - HB, nx) if offset < 0 else range(HB):
            gap = 0 if offset == 0 else nx - x if offset < 0 else x + 1
            edge = side if gap <= FAR else NEAR
            planes.append((x, x + HB + offset * nx, side - edge, ny + 2 * edge))
        slab = s + offset

        def fill(planes=planes, slab=slab):
            base = pl.multiple_of(slab * per_slab, 8)
            zrow = subs((nz, nz))
            yrow = subs((frame, nz))
            for g in range(groups):
                for p in range(part):
                    at = pl.ds((g * part + p) * nz, nz)
                    tile = disc[pl.ds(base + (g * 2 * part) // 8 * 8, 8), :]
                    r = (g * 2 * part) % 8 + p
                    key = tile[r : r + 1].astype(jnp.int32)
                    f = tile[r + part : r + part + 1]
                    z = key & (nz - 1)
                    y = (key >> log2(nz)) & (ny - 1)
                    x = (key >> log2(nz * ny)) & (nx - 1)
                    o = key >> log2(nz * ny * nx)
                    row = (o - t) * ny + y + side
                    in_row = jnp.where(yrow == row, 1.0, 0.0)
                    place = jnp.broadcast_to(x, (8, nz))
                    to = 0
                    for plane, _, first, count in planes:
                        here = place == plane
                        parts = [
                            jnp.where(here, in_row[first + k : first + k + 8], 0.0)
                            for k in range(0, count, 8)
                        ]
                        hot[pl.ds(to, count), at] = jnp.concatenate(parts, 0).astype(BF16)
                        to += count
                    hi = f.astype(BF16).astype(F32)
                    here = zrow == z
                    for q, part_of in enumerate((hi, f - hi)):
                        val[pl.ds(q * nz, nz), at] = jnp.where(here, part_of, 0.0).astype(BF16)
            total = sum(count for _, _, _, count in planes)
            got = lax.dot_general(
                hot[pl.ds(0, total), pl.ds(0, cols)],
                val[:, pl.ds(0, cols)],
                (((1,), (1,)), ((), ())),
                preferred_element_type=F32,
            )
            got = got[:, :nz] + got[:, nz:]
            at = 0
            for _, to, first, count in planes:
                out[to, pl.ds(first, count), :] = got[at : at + count]
                at += count

        if offset == 0:
            fill()
        else:
            inside = slab >= 0 if offset < 0 else slab < slabs
            pl.when(inside)(fill)

            @pl.when(jnp.logical_not(inside))
            def _(planes=planes):
                for _, to, first, count in planes:
                    out[to, pl.ds(first, count), :] = jnp.zeros((count, nz), F32)


def pre_kernel(
    rhs, dens, xa, xb, ya, yb, ca, cb, source,
    slots, v0, b0, w0, cx0, cy0, cp0, v1, b1, w1, cx1, cy1, cp1,
    rho0, dg0, u0, rho1, dg1, u1, tmp0, tmp1,
):
    nx, ny, nz = rhs.shape
    s, t = lax.axis_index("stream"), lax.axis_index("trans")
    groups = lax.axis_size("trans")
    s_even, t_even = s % 2 == 0, t % 2 == 0
    own = R0 + HALO
    full = nx + 2 * HALO
    zero0 = jnp.zeros((ROWS0, nz), F32)
    for i in range(full):
        rho0[i] = zero0
        b0[i] = zero0
    for i in range(nx):
        b0[HALO + i, pl.ds(own, ny), :] = rhs[i]
        rho0[HALO + i, pl.ds(own, ny), :] = dens[i]

    def sides(a, b):
        low = jnp.where(t_even, b, a)
        high = jnp.where(t_even, a, b)
        return jnp.where(t > 0, low, 0.0), jnp.where(t < groups - 1, high, 0.0)

    def near(ref, i, a, b):
        low, high = sides(a, b)
        ref[i, pl.ds(own - NEAR, NEAR), :] = low
        ref[i, pl.ds(own + ny, NEAR), :] = high

    def far(i, a, b):
        low, high = sides(a, b)
        b0[i, pl.ds(own - NEAR - FAR, FAR), :] = low[:FAR]
        b0[i, pl.ds(own + ny + NEAR, FAR), :] = high[:FAR]
        rho0[i, pl.ds(own - NEAR - FAR, FAR), :] = low[FAR:]
        rho0[i, pl.ds(own + ny + NEAR, FAR), :] = high[FAR:]

    for i in range(nx):
        near(b0, HALO + i, ya[i], yb[i])
        near(rho0, HALO + i, ya[nx + i], yb[nx + i])
        far(HALO + i, ya[2 * nx + i], yb[2 * nx + i])
    base = 0
    for x, high in ((xa, s_even), (xb, jnp.logical_not(s_even))):
        at = base
        for ref, first, count in ((b0, 0, HB), (rho0, HB, HD)):
            to = jnp.where(high, HALO + nx, HALO - count)
            for i in range(count):
                ref[to + i, pl.ds(own, ny), :] = x[first + i]
            to = jnp.where(high, HALO + nx, HALO - count + THIN)
            for i in range(count - THIN):
                near(ref, to + i, ca[at], cb[at])
                at += 1
        for i in range(THIN):
            low, top = sides(ca[at], cb[at])
            at += 1
            for ref, count, part in ((b0, HB, 0), (rho0, HD, FAR)):
                to = jnp.where(high, HALO + nx + count - THIN + i, HALO - count + THIN - 1 - i)
                ref[to, pl.ds(own - FAR, FAR), :] = low[part : part + FAR]
                ref[to, pl.ds(own + ny, FAR), :] = top[part : part + FAR]
        to = jnp.where(high, HALO + nx, HALO - FAR)
        for i in range(FAR):
            far(to + i, ca[at + i], cb[at + i])
        base += CORNER
    wide = ny + 2 * HALO
    for i in range(nx + 2 * HB):
        at = HALO - HB + i
        gap = max(HALO - at, at - HALO - nx + 1)
        rows = pl.ds(0, ROWS0) if gap <= FAR else pl.ds(own - NEAR, ny + 2 * NEAR)
        b0[at, rows, :] = 0.5 * (b0[at, rows, :] + source[i, rows, :])

    f0 = (cx0, cy0, cp0)
    lo, hi = HALO - HB, HALO + nx + HB
    zero_row = jnp.zeros((1, nz), F32)
    for i in range(lo - 1, hi + 1):
        for ref in (u0, v0, cy0):
            ref[i, pl.ds(R0 - 1, 1), :] = zero_row
        for ref in (u0, v0):
            ref[i, pl.ds(R0 + wide, 1), :] = zero_row
    setup(rho0, f0, w0, dg0, lo, hi, R0, wide, 1)
    start(u0, b0, w0, lo, hi, R0, wide)
    inner, outer = HALO - 2, HALO + nx + 2
    for x0, x1, cut in ((lo + 1, inner, 4), (inner, outer, 0), (outer, hi - 1, 4)):
        sweep(u0, v0, b0, w0, f0, x0, x1, R0 + cut, wide - 2 * cut, 1)

    half = nx // 2 + HALO
    wide1 = 16
    zero1 = jnp.zeros((ROWS1, nz), F32)
    for i in range(half):
        for ref in (rho1, b1, u1, v1, cy1):
            ref[i] = zero1
    for i in range(half):
        tmp0[i] = zero0

    def rho_rows(i):
        return rho0[i, pl.ds(R0, wide), :]

    rows_to = SHIFT1
    coarsen(MEAN, rho_rows, rho1, tmp0, (2, 1, half - 2), wide, 1, rows_to)

    for x0, x1, cut in ((lo + 2, HALO - 4, 8), (HALO - 4, HALO + nx + 4, 4), (HALO + nx + 4, hi - 2, 8)):

        def res_rows(i, cut=cut):
            return residual(v0, b0, dg0, f0, i, R0 + cut, wide - 2 * cut, 1)

        pairs = (x0, x0 // 2, (x1 - x0) // 2)
        coarsen(DOWN, res_rows, b1, tmp0, pairs, wide - 2 * cut, 1, rows_to + cut // 2)
    f1 = (cx1, cy1, cp1)
    lo1, hi1 = (lo + 2) // 2, (hi - 2) // 2
    setup(rho1, f1, w1, dg1, lo1, hi1, R1, wide1, 2)
    start(u1, b1, w1, lo1, hi1, R1, wide1)
    sweep(u1, v1, b1, w1, f1, lo1 + 1, hi1 - 1, R1, wide1, 2)

    own1 = SHIFT1 + HALO // 2
    ny1 = ny // 2
    first1 = HALO // 2

    def packed(factor, fine):
        value = None
        for k in range(nx // 4):
            tmp1[k] = fine(first1 + 2 * k) + fine(first1 + 2 * k + 1)
        for k in range(nx // 4):
            total = tmp1[k, pl.ds(0, ny1 // 2, stride=2), :] + tmp1[k, pl.ds(1, ny1 // 2, stride=2), :]
            even = (lanes(total.shape) // 2) % 2 == 0
            total = total + jnp.where(even, up(total, 2), down(total, 2))
            turn = lanes(total.shape) % 4 == k
            value = jnp.where(turn, total, 0.0 if value is None else value)
        return factor * value

    rows2 = ny1 // 2
    slots[0, pl.ds(0, rows2), :] = packed(
        DOWN, lambda i: residual(v1, b1, dg1, f1, i, own1, ny1, 2)
    )
    slots[0, pl.ds(rows2, rows2), :] = packed(MEAN, lambda i: rho1[i, pl.ds(own1, ny1), :])
    slot = slots[0]

    def put(g):
        slots[g] = slot

    over(1, slots.shape[0], put)


class Coarse:
    def __init__(self, k, refs, planes, rows, mult, nz):
        self.rho, self.cx, self.cy, self.cp, self.w, self.dg, self.b, self.va, self.vb = refs
        self.planes, self.rows = planes, rows
        self.pitch, self.mult, self.st = 1 << k, mult >> k, mult << k
        lane = lanes((rows, nz))
        self.sub = (lane // self.pitch) % self.mult
        self.even_z = (lane // self.st) % 2 == 0
        self.first, self.last = lane < self.st, lane >= nz - self.st
        self.at = pl.ds(8, rows)

    def each(self, fn):
        over(1, 1 + self.planes, fn, 8, 4)

    def next_x(self, here, above):
        if self.mult == 1:
            return above
        far = down(above, (self.mult - 1) * self.pitch)
        return jnp.where(self.sub == self.mult - 1, far, up(here, self.pitch))

    def prev_x(self, here, below):
        if self.mult == 1:
            return below
        far = up(below, (self.mult - 1) * self.pitch)
        return jnp.where(self.sub == 0, far, down(here, self.pitch))

    def setup(self):
        rho, cx, cy, cp, at, n = self.rho, self.cx, self.cy, self.cp, self.at, self.rows
        cx[0, at, :] = face(self.next_x(rho[0, at, :], rho[1, at, :]))

        def plane(i):
            here = rho[i, at, :]
            fx, fy = pair(
                here + self.next_x(here, rho[i + 1, at, :]), here + rho[i, pl.ds(9, n), :]
            )
            fp, alone = pair(here + jnp.where(self.last, 0.0, up(here, self.st)), here)
            fm = jnp.where(self.first, alone, down(fp, self.st))
            return (
                (cx, (i, at), fx),
                (cy, (i, at), fy),
                (cy, (i, pl.ds(7, 1)), face(rho[i, pl.ds(8, 1), :])),
                (cp, (i, at), jnp.where(self.last, 0.0, fp)),
                (self.dg, (i, at), (fx + fy) + (fp + fm)),
            )

        self.each(plane)

        def diagonal(i):
            diag = self.prev_x(cx[i, at, :], cx[i - 1, at, :]) + cy[i, pl.ds(7, n), :]
            diag = self.dg[i, at, :] + diag
            return (self.dg, (i, at), diag), (self.w, (i, at), omega_factor / diag)

        self.each(diagonal)

    def beside(self, v, i):
        at, n = self.at, self.rows
        here = v[i, at, :]
        fx, fz = self.cx[i, at, :], self.cp[i, at, :]
        total = fx * self.next_x(here, v[i + 1, at, :])
        total = total + self.prev_x(fx * here, self.cx[i - 1, at, :] * v[i - 1, at, :])
        total = total + self.cy[i, at, :] * v[i, pl.ds(9, n), :]
        total = total + self.cy[i, pl.ds(7, n), :] * v[i, pl.ds(7, n), :]
        return here, total + (fz * up(here, self.st) + down(fz * here, self.st))

    def start(self):
        def plane(i):
            return ((self.va, (i, self.at), self.w[i, self.at, :] * self.b[i, self.at, :]),)

        self.each(plane)

    def smooth(self, n):
        for _ in range(n):

            def plane(i):
                here, total = self.beside(self.va, i)
                new = self.w[i, self.at, :] * (self.b[i, self.at, :] + total)
                return ((self.vb, (i, self.at), (1.0 - omega_factor) * here + new),)

            self.each(plane)
            self.va, self.vb = self.vb, self.va

    def residual(self, i):
        here, total = self.beside(self.va, i)
        return self.b[i, self.at, :] + (total - self.dg[i, self.at, :] * here)

    def coarsen(self, factor, fine, out, tmp):
        half = self.rows // 2

        def means(i):
            total = tmp[i, pl.ds(0, half, stride=2), :] + tmp[i, pl.ds(1, half, stride=2), :]
            even_x, even_z = self.sub[:half] % 2 == 0, self.even_z[:half]
            total = total + jnp.where(even_x, up(total, self.pitch), down(total, self.pitch))
            total = total + jnp.where(even_z, up(total, self.st), down(total, self.st))
            return ((out, (i, pl.ds(8, half)), factor * total),)

        self.each(lambda i: ((tmp, (i, pl.ds(0, self.rows)), fine(i)),))
        self.each(means)

    def correct(self, below, tmp):
        self.each(lambda i: doubled(tmp, i, 0, below.va[i, below.at, :]))
        self.each(
            lambda i: (
                (
                    self.va,
                    (i, self.at),
                    self.va[i, self.at, :] + tmp[i, pl.ds(0, self.rows), :],
                ),
            )
        )


def post_kernel(slots, v0, b0, w0, cx0, cy0, cp0, v1, b1, w1, cx1, cy1, cp1, out, *refs):
    nx, ny, nz = out.shape
    slabs, groups = lax.axis_size("stream"), lax.axis_size("trans")
    s, t = lax.axis_index("stream"), lax.axis_index("trans")
    gx, gy = nx // 4, ny // 4
    assert gx * (nz // 4) == nz
    rows = groups * gy
    levels = [Coarse(k, refs[9 * k : 9 * k + 9], slabs, rows >> k, gx, nz) for k in range(3)]
    tmp, e1, u1, x1, e0, u0, x0 = refs[27:]
    for c in levels:
        zero = jnp.zeros((c.rows + 16, nz), F32)

        def clear(i, group=(c.rho, c.va, c.vb), zero=zero):
            for ref in group:
                ref[i] = zero

        over(0, slabs + 2, clear)

    two, three, four = levels
    top = subs((8, nz)) < 4

    def unpack(sl):
        for pair in range(groups // 2):
            first = slots[sl * groups + 2 * pair]
            second = slots[sl * groups + 2 * pair + 1]
            to = pl.ds(8 + 8 * pair, 8)
            two.b[1 + sl, to, :] = jnp.where(top, first, pltpu.roll(second, 4, 0))
            two.rho[1 + sl, to, :] = jnp.where(top, pltpu.roll(first, 4, 0), second)

    over(0, slabs, unpack, 8, 2)
    two.setup()
    two.coarsen(MEAN, lambda i: two.rho[i, two.at, :], three.rho, tmp)
    three.setup()
    three.coarsen(MEAN, lambda i: three.rho[i, three.at, :], four.rho, tmp)
    four.setup()
    two.start()
    two.smooth(1)
    two.coarsen(DOWN, two.residual, three.b, tmp)
    three.start()
    three.smooth(1)
    three.coarsen(DOWN, three.residual, four.b, tmp)
    four.start()
    four.smooth(CSWEEPS - 1)
    three.correct(four, tmp)
    three.smooth(POST)
    two.correct(three, tmp)
    two.smooth(POST)

    f1 = (cx1, cy1, cp1)
    first1, nx1 = HALO // 2, nx // 2
    wide1 = 16
    for i in range(e1.shape[0]):
        e1[i] = jnp.zeros((ROWS1, nz), F32)
    zero_row = jnp.zeros((1, nz), F32)
    for i in range(u1.shape[0]):
        for ref in (u1, x1):
            ref[i, pl.ds(R1 - 1, 1), :] = zero_row
            ref[i, pl.ds(R1 + wide1, 1), :] = zero_row
    place = lanes((gy + 4, nz)) % gx
    around = [two.va[s + k, pl.ds(t * gy + 6, gy + 4), :] for k in range(3)]
    for k in range(gx + 4):
        plane, sub = around[(k + gx - 2) // gx], (k + gx - 2) % gx
        value = plane if sub == 0 else pltpu.roll(plane, nz - sub, 1)
        for m in range(1, gx):
            value = jnp.where(place == m, pltpu.roll(plane, (m - sub) % nz, 1) if m != sub else plane, value)
        doubled(e1, k, SHIFT1 + first1 - 4, value)
    rows1 = pl.ds(R1, wide1)
    for i in range(first1 - 3, first1 + nx1 + 3):
        u1[i, rows1, :] = v1[i, rows1, :] + e1[(i - first1 + 4) // 2, rows1, :]
    sweep(u1, x1, b1, w1, f1, first1 - 2, first1 + nx1 + 2, R1, wide1, 2)
    sweep(x1, u1, b1, w1, f1, first1 - 1, first1 + nx1 + 1, R1, wide1, 2)

    f0 = (cx0, cy0, cp0)
    own = R0 + HALO
    low, count = own - 4, ny + 8
    for k in range(nx1 + 2):
        value = u1[first1 - 1 + k, pl.ds(SHIFT1 + first1 - 4, ny // 2 + 8), :]
        doubled(e0, k, own - 8, value)
    for i in range(HALO - 2, HALO + nx + 2):
        rows0 = pl.ds(low, count)
        u0[i, rows0, :] = v0[i, rows0, :] + e0[(i - HALO + 2) // 2, rows0, :]
    sweep(u0, x0, b0, w0, f0, HALO - 1, HALO + nx + 1, low, count, 1)
    for i in range(nx):
        out[i] = swept(x0, b0, w0, f0, HALO + i, own, ny, 1)


def exchange(count, parity, open_ends):
    pairs = []
    for i in range(count):
        j = ((i + parity) ^ 1) - parity
        if 0 <= j < count:
            pairs.append((i, j))
        elif not open_ends:
            pairs.append((i, count - 1 - i))
    return pairs


def swap(value, axis, parity, open_ends):
    count = lax.axis_size(axis)
    return lax.ppermute(value, axis, exchange(count, parity, open_ends))


def gather(value):
    return lax.all_to_all(value, AXES, 0, 0, tiled=True)


def sds(*shape):
    return jax.ShapeDtypeStruct(shape, F32)


def body(rhs, vof, disc_owner, disc_cell, disc_force):
    nx, ny, nz = rhs.shape
    slabs, groups = lax.axis_size("stream"), lax.axis_size("trans")
    devices = slabs * groups
    rows = disc_cell.shape[1] // nz
    halo_x = sds(HB + HD, ny, nz)
    halo_y = sds(3 * nx, 8, nz)
    corner = sds(2 * CORNER, 8, nz)

    block, row = sds(nx, ny, nz), pltpu.VMEM((rows, nz), jnp.int32)
    rhs, dens, xa, xb, ya, yb, disc = pl.pallas_call(
        functools.partial(pack_kernel, devices),
        out_shape=(block, block, halo_x, halo_x, halo_y, halo_y, sds(devices * 2 * rows, nz)),
        in_specs=[pl.BlockSpec(memory_space=pltpu.MemorySpace.HBM)] * 5,
        scratch_shapes=[
            pltpu.VMEM((nx, ny, nz), jnp.int32),
            row,
            row,
            pltpu.VMEM((rows, nz), F32),
            pltpu.SemaphoreType.DMA((5,)),
        ],
        compiler_params=params(12),
        name="pack",
    )(
        *(
            pltpu.with_memory_space_constraint(x, pltpu.MemorySpace.HBM)
            for x in (
                rhs,
                vof,
                disc_owner.reshape(rows, nz),
                disc_cell.reshape(rows, nz),
                disc_force.reshape(rows, nz),
            )
        )
    )
    disc = gather(disc)
    xa = swap(xa, "stream", 0, True)
    xb = swap(xb, "stream", 1, True)
    ya = swap(ya, "trans", 0, False)
    yb = swap(yb, "trans", 1, False)
    ca, cb = pl.pallas_call(
        corner_kernel, out_shape=(corner, corner), compiler_params=params(8), name="corner"
    )(xa, xb)
    ca = swap(ca, "trans", 0, False)
    cb = swap(cb, "trans", 1, False)
    cols = groups * rows * nz
    source = pl.pallas_call(
        functools.partial(source_kernel, (nx, ny, nz)),
        out_shape=sds(nx + 2 * HB, ROWS0, nz),
        scratch_shapes=[
            pltpu.VMEM((nx * ROWS0, cols), BF16),
            pltpu.VMEM((2 * nz, cols), BF16),
        ],
        compiler_params=params(24),
        name="source",
    )(disc)
    full, half = nx + 2 * HALO, nx // 2 + HALO
    frame0, frame1 = sds(full, ROWS0, nz), sds(half, ROWS1, nz)
    s0, s1 = pltpu.VMEM(frame0.shape, F32), pltpu.VMEM(frame1.shape, F32)
    slots, *state = pl.pallas_call(
        pre_kernel,
        out_shape=(sds(devices, 8, nz), *([frame0] * 6), *([frame1] * 6)),
        scratch_shapes=[
            s0, s0, s0, s1, s1, s1,
            pltpu.VMEM((half, ROWS0, nz), F32), pltpu.VMEM((nx // 4, ny // 2, nz), F32),
        ],
        compiler_params=params(28),
        name="presmooth",
    )(rhs, dens, xa, xb, ya, yb, ca, cb, source)
    slots = gather(slots)
    gy = groups * ny // 4
    scratch = [pltpu.VMEM((slabs + 2, (gy >> k) + 16, nz), F32) for k in range(3) for _ in range(9)]
    scratch += [
        pltpu.VMEM((slabs + 2, gy, nz), F32),
        pltpu.VMEM((nx // 4 + 4, ROWS1, nz), F32),
        s1,
        s1,
        pltpu.VMEM((nx // 2 + 2, ROWS0, nz), F32),
        s0,
        s0,
    ]
    return pl.pallas_call(
        post_kernel,
        out_shape=sds(nx, ny, nz),
        scratch_shapes=scratch,
        compiler_params=params(32),
        name="postsmooth",
    )(slots, *state)


def solution(mesh):
    return jax.shard_map(
        body,
        mesh=mesh,
        in_specs=(
            P("stream", "trans", None),
            P("stream", "trans", None),
            P("stream", "trans", None),
            P("stream", "trans"),
            P("stream", "trans"),
        ),
        out_specs=P("stream", "trans", None),
        check_vma=False,
    )
```

```python
import functools

import jax
import jax.numpy as jnp
from jax import lax
from jax.experimental import pallas as pl
from jax.experimental.pallas import tpu as pltpu
from jax.sharding import PartitionSpec as P


POST = 2
CSWEEPS = 8

air_density = 0.0012
omega_factor = 0.8

F32 = jnp.float32
BF16 = jnp.bfloat16
AXES = ("stream", "trans")

HALO = 12
HB = 10
HD = 11
NEAR = 8
FAR = 4
THIN = 3
CORNER = HB + HD - THIN + FAR
R0 = 4
ROWS0 = 48
R1 = 12
ROWS1 = 40
SHIFT1 = 10


def params(mib):
    return pltpu.CompilerParams(vmem_limit_bytes=mib << 20)


def lanes(shape):
    return lax.broadcasted_iota(jnp.int32, shape, len(shape) - 1)


def subs(shape):
    return lax.broadcasted_iota(jnp.int32, shape, len(shape) - 2)


def log2(n):
    assert n & (n - 1) == 0
    return n.bit_length() - 1


def up(x, st):
    return pltpu.roll(x, x.shape[-1] - st, x.ndim - 1)


def down(x, st):
    return pltpu.roll(x, st, x.ndim - 1)


def over(lo, hi, fn, limit=64, step=4):
    def group(indices):
        stores = [store for i in indices for store in fn(i) or ()]
        for ref, index, value in stores:
            ref[index] = value

    if hi - lo <= limit:
        for i in range(lo, hi, step):
            group(range(i, min(i + step, hi)))
        return
    whole = (hi - lo) // step

    def chunk(k, carry):
        group([lo + k * step + j for j in range(step)])
        return carry

    lax.fori_loop(0, whole, chunk, 0)
    group(range(lo + whole * step, hi))


LEAST = 0.8 * air_density


MEAN = 0.125
DOWN = 4 * MEAN


def face(den):
    return 1.0 / jnp.maximum(den, LEAST)


def pair(a, b):
    a, b = jnp.maximum(a, LEAST), jnp.maximum(b, LEAST)
    both = 1.0 / (a * b)
    return both * b, both * a


def setup(rho, faces, w, dg, x0, x1, r0, nr, st):
    cx, cy, cp = faces
    nz = rho.shape[-1]
    rows = pl.ds(r0, nr)
    lane = lanes((nr, nz))
    first, last = lane < st, lane >= nz - st
    cx[x0 - 1, rows, :] = face(rho[x0 - 1, rows, :] + rho[x0, rows, :])

    def plane(i):
        here = rho[i, rows, :]
        fx, fy = pair(here + rho[i + 1, rows, :], here + rho[i, pl.ds(r0 + 1, nr), :])
        fp, alone = pair(here + jnp.where(last, 0.0, up(here, st)), here)
        fm = jnp.where(first, alone, down(fp, st))
        at = (i, rows)
        before = face(rho[i, pl.ds(r0 - 1, 1), :] + rho[i, pl.ds(r0, 1), :])
        return (
            (cy, (i, pl.ds(r0 - 1, 1)), before),
            (cx, at, fx),
            (cy, at, fy),
            (cp, at, jnp.where(last, 0.0, fp)),
            (dg, at, (fx + fy) + (fp + fm)),
        )

    over(x0, x1, plane, step=SETUP_STEP)

    def diagonal(i):
        at = (i, rows)
        diag = dg[at] + (cx[i - 1, rows, :] + cy[i, pl.ds(r0 - 1, nr), :])
        return (dg, at, diag), (w, at, jnp.where(rho[at] > 0.0, omega_factor / diag, 0.0))

    over(x0, x1, diagonal)


SETUP_STEP = 4


def beside(v, faces, i, r0, nr, st):
    cx, cy, cp = faces
    rows = pl.ds(r0, nr)
    here = v[i, rows, :]
    total = cx[i, rows, :] * v[i + 1, rows, :] + cx[i - 1, rows, :] * v[i - 1, rows, :]
    total = total + cy[i, rows, :] * v[i, pl.ds(r0 + 1, nr), :]
    total = total + cy[i, pl.ds(r0 - 1, nr), :] * v[i, pl.ds(r0 - 1, nr), :]
    fz = cp[i, rows, :]
    total = total + (fz * up(here, st) + down(fz * here, st))
    return here, total


def start(v, b, w, x0, x1, r0, nr):
    rows = pl.ds(r0, nr)

    def plane(i):
        return ((v, (i, rows), w[i, rows, :] * b[i, rows, :]),)

    over(x0, x1, plane)


def swept(v, b, w, faces, i, r0, nr, st):
    rows = pl.ds(r0, nr)
    here, total = beside(v, faces, i, r0, nr, st)
    return (1.0 - omega_factor) * here + w[i, rows, :] * (b[i, rows, :] + total)


def sweep(v, out, b, w, faces, x0, x1, r0, nr, st):
    def plane(i):
        return ((out, (i, pl.ds(r0, nr)), swept(v, b, w, faces, i, r0, nr, st)),)

    over(x0, x1, plane)


def residual(v, b, dg, faces, i, r0, nr, st):
    here, total = beside(v, faces, i, r0, nr, st)
    rows = pl.ds(r0, nr)
    return b[i, rows, :] + (total - dg[i, rows, :] * here)


def coarsen(factor, fine, out, tmp, pairs, nr, st, to):
    a0, c0, count = pairs
    half = nr // 2

    def planes(k):
        return ((tmp, (c0 + k, pl.ds(0, nr)), fine(a0 + 2 * k) + fine(a0 + 2 * k + 1)),)

    def means(k):
        c = c0 + k
        total = tmp[c, pl.ds(0, half, stride=2), :] + tmp[c, pl.ds(1, half, stride=2), :]
        even = (lanes(total.shape) // st) % 2 == 0
        total = total + jnp.where(even, up(total, st), down(total, st))
        return ((out, (c, pl.ds(to, half)), factor * total),)

    over(0, count, planes, step=2)
    over(0, count, means)


def doubled(ref, k, row, value):
    n = value.shape[0]
    ref[k, pl.ds(row, n, stride=2), :] = value
    ref[k, pl.ds(row + 1, n, stride=2), :] = value


def half_tile(a, b, upper):
    top = subs(a.shape) < FAR
    return jnp.where(
        upper,
        jnp.where(top, pltpu.roll(a, FAR, 0), b),
        jnp.where(top, a, pltpu.roll(b, FAR, 0)),
    )


def pack_kernel(groups, *refs):
    outside, (rhs, dens, xa, xb, ya, yb, disc) = refs[:5], refs[5:12]
    vof, owner, cell, force, sems = refs[12:]
    inside = (rhs, vof, owner, cell, force)
    copies = [
        pltpu.make_async_copy(a, b, sems.at[i]) for i, (a, b) in enumerate(zip(outside, inside))
    ]
    for copy in copies:
        copy.start()
    for copy in copies:
        copy.wait()
    nx, ny, nz = rhs.shape
    s_even = lax.axis_index("stream") % 2 == 0
    t_even = lax.axis_index("trans") % 2 == 0
    for i in range(nx):
        dens[i] = air_density + ((1.0 - air_density) / 1000.0) * vof[i].astype(F32)
    tail_b, tail_d = nx - HB, nx - HD
    for out, tail in ((xa, s_even), (xb, jnp.logical_not(s_even))):
        at_b, at_d = jnp.where(tail, tail_b, 0), jnp.where(tail, tail_d, 0)
        for i in range(HB):
            out[i] = rhs[at_b + i]
        for i in range(HD):
            out[HB + i] = dens[at_d + i]
    for i in range(nx):
        b, d = rhs[i], dens[i]
        mid_b, mid_d = b[FAR : FAR + 8], d[FAR : FAR + 8]
        for out, tail in ((ya, t_even), (yb, jnp.logical_not(t_even))):
            out[i] = jnp.where(tail, b[ny - NEAR :], b[:NEAR])
            out[nx + i] = jnp.where(tail, d[ny - NEAR :], d[:NEAR])
            out[2 * nx + i] = half_tile(mid_b, mid_d, jnp.logical_not(tail))
    key = (owner[...] * (nx * ny * nz) + cell[...]).astype(F32)
    rows = key.shape[0]
    values = jnp.concatenate([key, force[...]], axis=0)
    if 2 * rows < 8:
        values = jnp.concatenate([values] * (4 // rows), axis=0)
    for g in range(groups * 2 * rows // 8):
        disc[pl.ds(8 * g, 8), :] = values


def corner_kernel(xa, xb, ca, cb):
    ny = xa.shape[1]
    s_even = lax.axis_index("stream") % 2 == 0
    t_even = lax.axis_index("trans") % 2 == 0
    base = 0
    for x, high in ((xa, s_even), (xb, jnp.logical_not(s_even))):

        def rows(i):
            tile = x[i]
            low_rows, high_rows = tile[:NEAR], tile[ny - NEAR :]
            return jnp.where(t_even, high_rows, low_rows), jnp.where(t_even, low_rows, high_rows)

        at = base
        for first, count in ((0, HB), (HB, HD)):
            of = first + jnp.where(high, 0, THIN)
            for i in range(count - THIN):
                ca[at], cb[at] = rows(of + i)
                at += 1
        for i in range(THIN):
            b = rows(jnp.where(high, HB - THIN + i, THIN - 1 - i))
            d = rows(HB + jnp.where(high, HD - THIN + i, THIN - 1 - i))
            ca[at] = half_tile(b[0], d[0], t_even)
            cb[at] = half_tile(b[1], d[1], jnp.logical_not(t_even))
            at += 1
        at_b = jnp.where(high, 0, HB - FAR)
        at_d = jnp.where(high, HB, HB + HD - FAR)
        for i in range(FAR):
            mid_b = x[at_b + i, pl.ds(FAR, 8), :]
            mid_d = x[at_d + i, pl.ds(FAR, 8), :]
            ca[at + i] = half_tile(mid_b, mid_d, jnp.logical_not(t_even))
            cb[at + i] = half_tile(mid_b, mid_d, t_even)
        base += CORNER


def source_kernel(shape, disc, out, hot, val):
    nx, ny, nz = shape
    slabs, groups = lax.axis_size("stream"), lax.axis_size("trans")
    s, t = lax.axis_index("stream"), lax.axis_index("trans")
    per_slab = disc.shape[0] // slabs
    part = per_slab // groups // 2
    frame = out.shape[1]
    cols = part * groups * nz
    side = (frame - ny) // 2
    for offset in (-1, 0, 1):
        planes = []
        for x in range(nx) if offset == 0 else range(nx - HB, nx) if offset < 0 else range(HB):
            gap = 0 if offset == 0 else nx - x if offset < 0 else x + 1
            edge = side if gap <= FAR else NEAR
            planes.append((x, x + HB + offset * nx, side - edge, ny + 2 * edge))
        slab = s + offset

        def fill(planes=planes, slab=slab):
            base = pl.multiple_of(slab * per_slab, 8)
            zrow = subs((nz, nz))
            yrow = subs((frame, nz))
            for g in range(groups):
                for p in range(part):
                    at = pl.ds((g * part + p) * nz, nz)
                    tile = disc[pl.ds(base + (g * 2 * part) // 8 * 8, 8), :]
                    r = (g * 2 * part) % 8 + p
                    key = tile[r : r + 1].astype(jnp.int32)
                    f = tile[r + part : r + part + 1]
                    z = key & (nz - 1)
                    y = (key >> log2(nz)) & (ny - 1)
                    x = (key >> log2(nz * ny)) & (nx - 1)
                    o = key >> log2(nz * ny * nx)
                    row = (o - t) * ny + y + side
                    in_row = jnp.where(yrow == row, 1.0, 0.0)
                    place = jnp.broadcast_to(x, (8, nz))
                    to = 0
                    for plane, _, first, count in planes:
                        here = place == plane
                        parts = [
                            jnp.where(here, in_row[first + k : first + k + 8], 0.0)
                            for k in range(0, count, 8)
                        ]
                        hot[pl.ds(to, count), at] = jnp.concatenate(parts, 0).astype(BF16)
                        to += count
                    hi = f.astype(BF16).astype(F32)
                    here = zrow == z
                    for q, part_of in enumerate((hi, f - hi)):
                        val[pl.ds(q * nz, nz), at] = jnp.where(here, part_of, 0.0).astype(BF16)
            total = sum(count for _, _, _, count in planes)
            got = lax.dot_general(
                hot[pl.ds(0, total), pl.ds(0, cols)],
                val[:, pl.ds(0, cols)],
                (((1,), (1,)), ((), ())),
                preferred_element_type=F32,
            )
            got = got[:, :nz] + got[:, nz:]
            at = 0
            for _, to, first, count in planes:
                out[to, pl.ds(first, count), :] = got[at : at + count]
                at += count

        if offset == 0:
            fill()
        else:
            inside = slab >= 0 if offset < 0 else slab < slabs
            pl.when(inside)(fill)

            @pl.when(jnp.logical_not(inside))
            def _(planes=planes):
                for _, to, first, count in planes:
                    out[to, pl.ds(first, count), :] = jnp.zeros((count, nz), F32)


def pre_kernel(
    rhs, dens, xa, xb, ya, yb, ca, cb, source,
    slots, v0, b0, w0, cx0, cy0, cp0, v1, b1, w1, cx1, cy1, cp1,
    rho0, dg0, u0, rho1, dg1, u1, tmp0, tmp1,
):
    nx, ny, nz = rhs.shape
    s, t = lax.axis_index("stream"), lax.axis_index("trans")
    groups = lax.axis_size("trans")
    s_even, t_even = s % 2 == 0, t % 2 == 0
    own = R0 + HALO
    full = nx + 2 * HALO
    zero0 = jnp.zeros((ROWS0, nz), F32)
    for i in range(full):
        rho0[i] = zero0
        b0[i] = zero0
    for i in range(nx):
        b0[HALO + i, pl.ds(own, ny), :] = rhs[i]
        rho0[HALO + i, pl.ds(own, ny), :] = dens[i]

    def sides(a, b):
        low = jnp.where(t_even, b, a)
        high = jnp.where(t_even, a, b)
        return jnp.where(t > 0, low, 0.0), jnp.where(t < groups - 1, high, 0.0)

    def near(ref, i, a, b):
        low, high = sides(a, b)
        ref[i, pl.ds(own - NEAR, NEAR), :] = low
        ref[i, pl.ds(own + ny, NEAR), :] = high

    def far(i, a, b):
        low, high = sides(a, b)
        b0[i, pl.ds(own - NEAR - FAR, FAR), :] = low[:FAR]
        b0[i, pl.ds(own + ny + NEAR, FAR), :] = high[:FAR]
        rho0[i, pl.ds(own - NEAR - FAR, FAR), :] = low[FAR:]
        rho0[i, pl.ds(own + ny + NEAR, FAR), :] = high[FAR:]

    for i in range(nx):
        near(b0, HALO + i, ya[i], yb[i])
        near(rho0, HALO + i, ya[nx + i], yb[nx + i])
        far(HALO + i, ya[2 * nx + i], yb[2 * nx + i])
    base = 0
    for x, high in ((xa, s_even), (xb, jnp.logical_not(s_even))):
        at = base
        for ref, first, count in ((b0, 0, HB), (rho0, HB, HD)):
            to = jnp.where(high, HALO + nx, HALO - count)
            for i in range(count):
                ref[to + i, pl.ds(own, ny), :] = x[first + i]
            to = jnp.where(high, HALO + nx, HALO - count + THIN)
            for i in range(count - THIN):
                near(ref, to + i, ca[at], cb[at])
                at += 1
        for i in range(THIN):
            low, top = sides(ca[at], cb[at])
            at += 1
            for ref, count, part in ((b0, HB, 0), (rho0, HD, FAR)):
                to = jnp.where(high, HALO + nx + count - THIN + i, HALO - count + THIN - 1 - i)
                ref[to, pl.ds(own - FAR, FAR), :] = low[part : part + FAR]
                ref[to, pl.ds(own + ny, FAR), :] = top[part : part + FAR]
        to = jnp.where(high, HALO + nx, HALO - FAR)
        for i in range(FAR):
            far(to + i, ca[at + i], cb[at + i])
        base += CORNER
    wide = ny + 2 * HALO
    for i in range(nx + 2 * HB):
        at = HALO - HB + i
        gap = max(HALO - at, at - HALO - nx + 1)
        rows = pl.ds(0, ROWS0) if gap <= FAR else pl.ds(own - NEAR, ny + 2 * NEAR)
        b0[at, rows, :] = 0.5 * (b0[at, rows, :] + source[i, rows, :])

    f0 = (cx0, cy0, cp0)
    lo, hi = HALO - HB, HALO + nx + HB
    zero_row = jnp.zeros((1, nz), F32)
    for i in range(lo - 1, hi + 1):
        for ref in (u0, v0, cy0):
            ref[i, pl.ds(R0 - 1, 1), :] = zero_row
        for ref in (u0, v0):
            ref[i, pl.ds(R0 + wide, 1), :] = zero_row
    setup(rho0, f0, w0, dg0, lo, hi, R0, wide, 1)
    start(u0, b0, w0, lo, hi, R0, wide)
    inner, outer = HALO - 2, HALO + nx + 2
    for x0, x1, cut in ((lo + 1, inner, 4), (inner, outer, 0), (outer, hi - 1, 4)):
        sweep(u0, v0, b0, w0, f0, x0, x1, R0 + cut, wide - 2 * cut, 1)

    half = nx // 2 + HALO
    wide1 = 16

    def rho_rows(i):
        return rho0[i, pl.ds(R0, wide), :]

    rows_to = SHIFT1
    coarsen(MEAN, rho_rows, rho1, tmp0, (2, 1, half - 2), wide, 1, rows_to)

    for x0, x1, cut in ((lo + 2, HALO - 4, 8), (HALO - 4, HALO + nx + 4, 4), (HALO + nx + 4, hi - 2, 8)):

        def res_rows(i, cut=cut):
            return residual(v0, b0, dg0, f0, i, R0 + cut, wide - 2 * cut, 1)

        pairs = (x0, x0 // 2, (x1 - x0) // 2)
        coarsen(DOWN, res_rows, b1, tmp0, pairs, wide - 2 * cut, 1, rows_to + cut // 2)
    f1 = (cx1, cy1, cp1)
    lo1, hi1 = (lo + 2) // 2, (hi - 2) // 2
    setup(rho1, f1, w1, dg1, lo1, hi1, R1, wide1, 2)
    start(u1, b1, w1, lo1, hi1, R1, wide1)
    sweep(u1, v1, b1, w1, f1, lo1 + 1, hi1 - 1, R1, wide1, 2)

    own1 = SHIFT1 + HALO // 2
    ny1 = ny // 2
    first1 = HALO // 2

    def packed(factor, fine):
        value = None
        for k in range(nx // 4):
            tmp1[k] = fine(first1 + 2 * k) + fine(first1 + 2 * k + 1)
        for k in range(nx // 4):
            total = tmp1[k, pl.ds(0, ny1 // 2, stride=2), :] + tmp1[k, pl.ds(1, ny1 // 2, stride=2), :]
            even = (lanes(total.shape) // 2) % 2 == 0
            total = total + jnp.where(even, up(total, 2), down(total, 2))
            turn = lanes(total.shape) % 4 == k
            value = jnp.where(turn, total, 0.0 if value is None else value)
        return factor * value

    rows2 = ny1 // 2
    slots[0, pl.ds(0, rows2), :] = packed(
        DOWN, lambda i: residual(v1, b1, dg1, f1, i, own1, ny1, 2)
    )
    slots[0, pl.ds(rows2, rows2), :] = packed(MEAN, lambda i: rho1[i, pl.ds(own1, ny1), :])
    slot = slots[0]

    def put(g):
        slots[g] = slot

    over(1, slots.shape[0], put)


class Coarse:
    def __init__(self, k, refs, planes, rows, mult, nz):
        self.rho, self.cx, self.cy, self.cp, self.w, self.dg, self.b, self.va, self.vb = refs
        self.planes, self.rows = planes, rows
        self.pitch, self.mult, self.st = 1 << k, mult >> k, mult << k
        lane = lanes((rows, nz))
        self.sub = (lane // self.pitch) % self.mult
        self.even_z = (lane // self.st) % 2 == 0
        self.first, self.last = lane < self.st, lane >= nz - self.st
        self.at = pl.ds(8, rows)

    def each(self, fn):
        over(1, 1 + self.planes, fn, 8, 4)

    def next_x(self, here, above):
        if self.mult == 1:
            return above
        far = down(above, (self.mult - 1) * self.pitch)
        return jnp.where(self.sub == self.mult - 1, far, up(here, self.pitch))

    def prev_x(self, here, below):
        if self.mult == 1:
            return below
        far = up(below, (self.mult - 1) * self.pitch)
        return jnp.where(self.sub == 0, far, down(here, self.pitch))

    def setup(self):
        rho, cx, cy, cp, at, n = self.rho, self.cx, self.cy, self.cp, self.at, self.rows
        cx[0, at, :] = face(self.next_x(rho[0, at, :], rho[1, at, :]))

        def plane(i):
            here = rho[i, at, :]
            fx, fy = pair(
                here + self.next_x(here, rho[i + 1, at, :]), here + rho[i, pl.ds(9, n), :]
            )
            fp, alone = pair(here + jnp.where(self.last, 0.0, up(here, self.st)), here)
            fm = jnp.where(self.first, alone, down(fp, self.st))
            return (
                (cx, (i, at), fx),
                (cy, (i, at), fy),
                (cy, (i, pl.ds(7, 1)), face(rho[i, pl.ds(8, 1), :])),
                (cp, (i, at), jnp.where(self.last, 0.0, fp)),
                (self.dg, (i, at), (fx + fy) + (fp + fm)),
            )

        self.each(plane)

        def diagonal(i):
            diag = self.prev_x(cx[i, at, :], cx[i - 1, at, :]) + cy[i, pl.ds(7, n), :]
            diag = self.dg[i, at, :] + diag
            return (self.dg, (i, at), diag), (self.w, (i, at), omega_factor / diag)

        self.each(diagonal)

    def beside(self, v, i):
        at, n = self.at, self.rows
        here = v[i, at, :]
        fx, fz = self.cx[i, at, :], self.cp[i, at, :]
        total = fx * self.next_x(here, v[i + 1, at, :])
        total = total + self.prev_x(fx * here, self.cx[i - 1, at, :] * v[i - 1, at, :])
        total = total + self.cy[i, at, :] * v[i, pl.ds(9, n), :]
        total = total + self.cy[i, pl.ds(7, n), :] * v[i, pl.ds(7, n), :]
        return here, total + (fz * up(here, self.st) + down(fz * here, self.st))

    def start(self):
        def plane(i):
            return ((self.va, (i, self.at), self.w[i, self.at, :] * self.b[i, self.at, :]),)

        self.each(plane)

    def smooth(self, n):
        for _ in range(n):

            def plane(i):
                here, total = self.beside(self.va, i)
                new = self.w[i, self.at, :] * (self.b[i, self.at, :] + total)
                return ((self.vb, (i, self.at), (1.0 - omega_factor) * here + new),)

            self.each(plane)
            self.va, self.vb = self.vb, self.va

    def residual(self, i):
        here, total = self.beside(self.va, i)
        return self.b[i, self.at, :] + (total - self.dg[i, self.at, :] * here)

    def coarsen(self, factor, fine, out, tmp):
        half = self.rows // 2

        def means(i):
            total = tmp[i, pl.ds(0, half, stride=2), :] + tmp[i, pl.ds(1, half, stride=2), :]
            even_x, even_z = self.sub[:half] % 2 == 0, self.even_z[:half]
            total = total + jnp.where(even_x, up(total, self.pitch), down(total, self.pitch))
            total = total + jnp.where(even_z, up(total, self.st), down(total, self.st))
            return ((out, (i, pl.ds(8, half)), factor * total),)

        self.each(lambda i: ((tmp, (i, pl.ds(0, self.rows)), fine(i)),))
        self.each(means)

    def correct(self, below, tmp):
        self.each(lambda i: doubled(tmp, i, 0, below.va[i, below.at, :]))
        self.each(
            lambda i: (
                (
                    self.va,
                    (i, self.at),
                    self.va[i, self.at, :] + tmp[i, pl.ds(0, self.rows), :],
                ),
            )
        )


def post_kernel(slots, v0, b0, w0, cx0, cy0, cp0, v1, b1, w1, cx1, cy1, cp1, out, *refs):
    nx, ny, nz = out.shape
    slabs, groups = lax.axis_size("stream"), lax.axis_size("trans")
    s, t = lax.axis_index("stream"), lax.axis_index("trans")
    gx, gy = nx // 4, ny // 4
    assert gx * (nz // 4) == nz
    rows = groups * gy
    levels = [Coarse(k, refs[9 * k : 9 * k + 9], slabs, rows >> k, gx, nz) for k in range(3)]
    tmp, e1, u1, x1, e0, u0, x0 = refs[27:]
    for c in levels:
        zero = jnp.zeros((c.rows + 16, nz), F32)

        def clear(i, group=(c.rho, c.va, c.vb), zero=zero):
            for ref in group:
                ref[i] = zero

        over(0, slabs + 2, clear)

    two, three, four = levels
    top = subs((8, nz)) < 4

    def unpack(sl):
        for pair in range(groups // 2):
            first = slots[sl * groups + 2 * pair]
            second = slots[sl * groups + 2 * pair + 1]
            to = pl.ds(8 + 8 * pair, 8)
            two.b[1 + sl, to, :] = jnp.where(top, first, pltpu.roll(second, 4, 0))
            two.rho[1 + sl, to, :] = jnp.where(top, pltpu.roll(first, 4, 0), second)

    over(0, slabs, unpack, 8, 2)
    two.setup()
    two.coarsen(MEAN, lambda i: two.rho[i, two.at, :], three.rho, tmp)
    three.setup()
    three.coarsen(MEAN, lambda i: three.rho[i, three.at, :], four.rho, tmp)
    four.setup()
    two.start()
    two.smooth(1)
    two.coarsen(DOWN, two.residual, three.b, tmp)
    three.start()
    three.smooth(1)
    three.coarsen(DOWN, three.residual, four.b, tmp)
    four.start()
    four.smooth(CSWEEPS - 1)
    three.correct(four, tmp)
    three.smooth(POST)
    two.correct(three, tmp)
    two.smooth(POST)

    f1 = (cx1, cy1, cp1)
    first1, nx1 = HALO // 2, nx // 2
    wide1 = 16
    zero_row = jnp.zeros((1, nz), F32)
    for i in range(u1.shape[0]):
        for ref in (u1, x1):
            ref[i, pl.ds(R1 - 1, 1), :] = zero_row
            ref[i, pl.ds(R1 + wide1, 1), :] = zero_row
    place = lanes((gy + 4, nz)) % gx
    around = [two.va[s + k, pl.ds(t * gy + 6, gy + 4), :] for k in range(3)]
    for k in range(gx + 4):
        plane, sub = around[(k + gx - 2) // gx], (k + gx - 2) % gx
        value = plane if sub == 0 else pltpu.roll(plane, nz - sub, 1)
        for m in range(1, gx):
            value = jnp.where(place == m, pltpu.roll(plane, (m - sub) % nz, 1) if m != sub else plane, value)
        doubled(e1, k, SHIFT1 + first1 - 4, value)
    rows1 = pl.ds(R1, wide1)
    for i in range(first1 - 3, first1 + nx1 + 3):
        u1[i, rows1, :] = v1[i, rows1, :] + e1[(i - first1 + 4) // 2, rows1, :]
    sweep(u1, x1, b1, w1, f1, first1 - 2, first1 + nx1 + 2, R1, wide1, 2)
    sweep(x1, u1, b1, w1, f1, first1 - 1, first1 + nx1 + 1, R1, wide1, 2)

    f0 = (cx0, cy0, cp0)
    own = R0 + HALO
    low, count = own - 4, ny + 8
    for k in range(nx1 + 2):
        value = u1[first1 - 1 + k, pl.ds(SHIFT1 + first1 - 4, ny // 2 + 8), :]
        doubled(e0, k, own - 8, value)
    for i in range(HALO - 2, HALO + nx + 2):
        rows0 = pl.ds(low, count)
        u0[i, rows0, :] = v0[i, rows0, :] + e0[(i - HALO + 2) // 2, rows0, :]
    sweep(u0, x0, b0, w0, f0, HALO - 1, HALO + nx + 1, low, count, 1)
    for i in range(nx):
        out[i] = swept(x0, b0, w0, f0, HALO + i, own, ny, 1)


def exchange(count, parity, open_ends):
    pairs = []
    for i in range(count):
        j = ((i + parity) ^ 1) - parity
        if 0 <= j < count:
            pairs.append((i, j))
        elif not open_ends:
            pairs.append((i, count - 1 - i))
    return pairs


def swap(value, axis, parity, open_ends):
    count = lax.axis_size(axis)
    return lax.ppermute(value, axis, exchange(count, parity, open_ends))


def gather(value):
    return lax.all_to_all(value, AXES, 0, 0, tiled=True)


def sds(*shape):
    return jax.ShapeDtypeStruct(shape, F32)


def body(rhs, vof, disc_owner, disc_cell, disc_force):
    nx, ny, nz = rhs.shape
    slabs, groups = lax.axis_size("stream"), lax.axis_size("trans")
    devices = slabs * groups
    rows = disc_cell.shape[1] // nz
    halo_x = sds(HB + HD, ny, nz)
    halo_y = sds(3 * nx, 8, nz)
    corner = sds(2 * CORNER, 8, nz)

    block, row = sds(nx, ny, nz), pltpu.VMEM((rows, nz), jnp.int32)
    rhs, dens, xa, xb, ya, yb, disc = pl.pallas_call(
        functools.partial(pack_kernel, devices),
        out_shape=(block, block, halo_x, halo_x, halo_y, halo_y, sds(devices * 2 * rows, nz)),
        in_specs=[pl.BlockSpec(memory_space=pltpu.MemorySpace.HBM)] * 5,
        scratch_shapes=[
            pltpu.VMEM((nx, ny, nz), jnp.int32),
            row,
            row,
            pltpu.VMEM((rows, nz), F32),
            pltpu.SemaphoreType.DMA((5,)),
        ],
        compiler_params=params(12),
        name="pack",
    )(
        *(
            pltpu.with_memory_space_constraint(x, pltpu.MemorySpace.HBM)
            for x in (
                rhs,
                vof,
                disc_owner.reshape(rows, nz),
                disc_cell.reshape(rows, nz),
                disc_force.reshape(rows, nz),
            )
        )
    )
    disc = gather(disc)
    xa = swap(xa, "stream", 0, True)
    xb = swap(xb, "stream", 1, True)
    ya = swap(ya, "trans", 0, False)
    yb = swap(yb, "trans", 1, False)
    ca, cb = pl.pallas_call(
        corner_kernel, out_shape=(corner, corner), compiler_params=params(8), name="corner"
    )(xa, xb)
    ca = swap(ca, "trans", 0, False)
    cb = swap(cb, "trans", 1, False)
    cols = groups * rows * nz
    source = pl.pallas_call(
        functools.partial(source_kernel, (nx, ny, nz)),
        out_shape=sds(nx + 2 * HB, ROWS0, nz),
        scratch_shapes=[
            pltpu.VMEM((nx * ROWS0, cols), BF16),
            pltpu.VMEM((2 * nz, cols), BF16),
        ],
        compiler_params=params(24),
        name="source",
    )(disc)
    full, half = nx + 2 * HALO, nx // 2 + HALO
    frame0, frame1 = sds(full, ROWS0, nz), sds(half, ROWS1, nz)
    s0, s1 = pltpu.VMEM(frame0.shape, F32), pltpu.VMEM(frame1.shape, F32)
    slots, *state = pl.pallas_call(
        pre_kernel,
        out_shape=(sds(devices, 8, nz), *([frame0] * 6), *([frame1] * 6)),
        scratch_shapes=[
            s0, s0, s0, s1, s1, s1,
            pltpu.VMEM((half, ROWS0, nz), F32), pltpu.VMEM((nx // 4, ny // 2, nz), F32),
        ],
        compiler_params=params(28),
        name="presmooth",
    )(rhs, dens, xa, xb, ya, yb, ca, cb, source)
    slots = gather(slots)
    gy = groups * ny // 4
    scratch = [pltpu.VMEM((slabs + 2, (gy >> k) + 16, nz), F32) for k in range(3) for _ in range(9)]
    scratch += [
        pltpu.VMEM((slabs + 2, gy, nz), F32),
        pltpu.VMEM((nx // 4 + 4, ROWS1, nz), F32),
        s1,
        s1,
        pltpu.VMEM((nx // 2 + 2, ROWS0, nz), F32),
        s0,
        s0,
    ]
    return pl.pallas_call(
        post_kernel,
        out_shape=sds(nx, ny, nz),
        scratch_shapes=scratch,
        compiler_params=params(32),
        name="postsmooth",
    )(slots, *state)


def solution(mesh):
    return jax.shard_map(
        body,
        mesh=mesh,
        in_specs=(
            P("stream", "trans", None),
            P("stream", "trans", None),
            P("stream", "trans", None),
            P("stream", "trans"),
            P("stream", "trans"),
        ),
        out_specs=P("stream", "trans", None),
        check_vma=False,
    )
```
